32 devices in a mesh: fsdp: 4 (over x, core), heads: 2 (over y), tensor: 4 (over z).
Axes of the slice: x: 2, y: 2, z: 4, core: 2. Of those that a mesh axis runs over, the one named last changes fastest.
Arguments:
- latent_tokens: bfloat16 [8, 1024, 1536], P('fsdp', 'heads'), may hold values from -6 to 6
- prompt_tokens: bfloat16 [8, 154, 1536], P('fsdp', 'heads'), may hold values from -6 to 6
- conditioning: bfloat16 [8, 1536], P('fsdp'), may hold values from -6 to 6
- latent_modulation: bfloat16 [1536, 6, 1536], P(('fsdp', 'heads'), None, 'tensor'), may hold values from -0.15625 to 0.15625
- prompt_modulation: bfloat16 [1536, 6, 1536], P(('fsdp', 'heads'), None, 'tensor'), may hold values from -0.15625 to 0.15625
- latent_modulation_bias: bfloat16 [6, 1536], P(None, 'tensor'), may hold values from -3 to 3
- prompt_modulation_bias: bfloat16 [6, 1536], P(None, 'tensor'), may hold values from -3 to 3
- latent_attention: bfloat16 [1536, 3, 1536], P(('fsdp', 'heads'), None, 'tensor'), may hold values from -0.15625 to 0.15625
- prompt_attention: bfloat16 [1536, 3, 1536], P(('fsdp', 'heads'), None, 'tensor'), may hold values from -0.15625 to 0.15625
- latent_attention_bias: bfloat16 [2, 1536], P(None, 'tensor'), may hold values from -3 to 3
- prompt_attention_bias: bfloat16 [2, 1536], P(None, 'tensor'), may hold values from -3 to 3
- latent_projection: bfloat16 [1536, 1536], P(('fsdp', 'heads'), 'tensor'), may hold values from -0.875 to 0.875
- prompt_projection: bfloat16 [1536, 1536], P(('fsdp', 'heads'), 'tensor'), may hold values from -0.875 to 0.875
- latent_projection_bias: bfloat16 [1536], P(('fsdp', 'heads')), may hold values from -3 to 3
- prompt_projection_bias: bfloat16 [1536], P(('fsdp', 'heads')), may hold values from -3 to 3
- latent_expand: bfloat16 [1536, 6144], P(('fsdp', 'heads'), 'tensor'), may hold values from -0.15625 to 0.15625
- prompt_expand: bfloat16 [1536, 6144], P(('fsdp', 'heads'), 'tensor'), may hold values from -0.15625 to 0.15625
- latent_expand_bias: bfloat16 [6144], P('tensor'), may hold values from -3 to 3
- prompt_expand_bias: bfloat16 [6144], P('tensor'), may hold values from -3 to 3
- latent_contract: bfloat16 [1536, 6144], P(('fsdp', 'heads'), 'tensor'), may hold values from -0.078125 to 0.078125
- prompt_contract: bfloat16 [1536, 6144], P(('fsdp', 'heads'), 'tensor'), may hold values from -0.078125 to 0.078125
- latent_contract_bias: bfloat16 [1536], P(('fsdp', 'heads')), may hold values from -3 to 3
- prompt_contract_bias: bfloat16 [1536], P(('fsdp', 'heads')), may hold values from -3 to 3
- latent_cotangent: bfloat16 [8, 1024, 1536], P('fsdp', 'heads'), may hold values from -6 to 6
- prompt_cotangent: bfloat16 [8, 154, 1536], P('fsdp', 'heads'), may hold values from -6 to 6
Outputs:
- latent_result: bfloat16 [8, 1024, 1536], P('fsdp', 'heads')
- prompt_result: bfloat16 [8, 154, 1536], P('fsdp', 'heads')
- latent_gradient: float32 [8, 1024, 1536], P('fsdp', 'heads')
- prompt_gradient: float32 [8, 154, 1536], P('fsdp', 'heads')
- conditioning_gradient: float32 [8, 1536], P('fsdp')
- latent_modulation_gradient: float32 [1536, 6, 1536], P(('fsdp', 'heads'), None, 'tensor')
- prompt_modulation_gradient: float32 [1536, 6, 1536], P(('fsdp', 'heads'), None, 'tensor')
- latent_modulation_bias_gradient: float32 [6, 1536], P(None, 'tensor')
- prompt_modulation_bias_gradient: float32 [6, 1536], P(None, 'tensor')
- latent_attention_gradient: float32 [1536, 3, 1536], P(('fsdp', 'heads'), None, 'tensor')
- prompt_attention_gradient: float32 [1536, 3, 1536], P(('fsdp', 'heads'), None, 'tensor')
- latent_attention_bias_gradient: float32 [2, 1536], P(None, 'tensor')
- prompt_attention_bias_gradient: float32 [2, 1536], P(None, 'tensor')
- latent_projection_gradient: float32 [1536, 1536], P(('fsdp', 'heads'), 'tensor')
- prompt_projection_gradient: float32 [1536, 1536], P(('fsdp', 'heads'), 'tensor')
- latent_projection_bias_gradient: float32 [1536], P(('fsdp', 'heads'))
- prompt_projection_bias_gradient: float32 [1536], P(('fsdp', 'heads'))
- latent_expand_gradient: float32 [1536, 6144], P(('fsdp', 'heads'), 'tensor')
- prompt_expand_gradient: float32 [1536, 6144], P(('fsdp', 'heads'), 'tensor')
- latent_expand_bias_gradient: float32 [6144], P('tensor')
- prompt_expand_bias_gradient: float32 [6144], P('tensor')
- latent_contract_gradient: float32 [1536, 6144], P(('fsdp', 'heads'), 'tensor')
- prompt_contract_gradient: float32 [1536, 6144], P(('fsdp', 'heads'), 'tensor')
- latent_contract_bias_gradient: float32 [1536], P(('fsdp', 'heads'))
- prompt_contract_bias_gradient: float32 [1536], P(('fsdp', 'heads'))
The draws below stay inside these ranges and needn't reach their ends.
All inputs are finite; a program needn't handle non-finite values.
Results may differ from the reference program's by a relative error of at most 0.013.
The reference program's roundings to bfloat16 on the way count: a program that leaves them out, or rounds other values in their place, can miss the bound.
Values may be sent and summed in bfloat16 or wider, within the bound.
A program may use at most 256 MiB of HBM per device.

```python
import jax
import jax.numpy as jnp
from jax import lax

D = 1536
HEADS = 24
HD = 64
FF = 6144
IMG = 1024
TXT = 154
SEQS = 8


def steps_of(rng, shape, pieces, least, largest):
    factor_of, own = 1.0, jax.random.fold_in(rng, 6)
    for dim, shards_of in pieces:
        steps = jnp.exp(jax.random.uniform(jax.random.fold_in(own, dim), (shards_of,), jnp.float32, least / len(pieces), largest / len(pieces)))
        factor_of = factor_of * jnp.repeat(steps, shape[dim] // shards_of).reshape([-1 if axis == dim else 1 for axis in range(len(shape))])
    return factor_of


def gaussian(key, shape, width, reach, cuts=(), kind=jnp.bfloat16):
    level = steps_of(key, shape, cuts, -0.22, 0.18) if cuts else 1.0
    array = jax.random.normal(key, shape, jnp.float32) * width * level
    return jnp.minimum(jnp.maximum(array, -reach), reach).astype(kind)


def setup_inputs(seed: int = 0) -> dict:
    arg_keys = jax.random.split(jax.random.key(seed), 26)
    return {
        "latent_tokens": gaussian(arg_keys[0], (SEQS, IMG, D), 1.0, 6.0, ((0, 4), (1, 2))),
        "prompt_tokens": gaussian(arg_keys[1], (SEQS, TXT, D), 1.0, 6.0, ((0, 4), (1, 2))),
        "conditioning": gaussian(arg_keys[2], (SEQS, D), 1.0, 6.0, ((0, 4),)),
        "latent_modulation": gaussian(arg_keys[3], (D, 6, D), D ** -0.5, 0.15625, ((0, 8), (2, 4))),
        "prompt_modulation": gaussian(arg_keys[4], (D, 6, D), D ** -0.5, 0.15625, ((0, 8), (2, 4))),
        "latent_modulation_bias": gaussian(arg_keys[5], (6, D), 0.5, 3.0, ((1, 4),)),
        "prompt_modulation_bias": gaussian(arg_keys[6], (6, D), 0.5, 3.0, ((1, 4),)),
        "latent_attention": gaussian(arg_keys[7], (D, 3, D), D ** -0.5, 0.15625, ((0, 8), (2, 4))),
        "prompt_attention": gaussian(arg_keys[8], (D, 3, D), D ** -0.5, 0.15625, ((0, 8), (2, 4))),
        "latent_attention_bias": gaussian(arg_keys[9], (2, D), 0.5, 3.0, ((1, 4),)),
        "prompt_attention_bias": gaussian(arg_keys[10], (2, D), 0.5, 3.0, ((1, 4),)),
        "latent_projection": gaussian(arg_keys[11], (D, D), (D // 32) ** -0.5, 0.875, ((0, 8), (1, 4))),
        "prompt_projection": gaussian(arg_keys[12], (D, D), (D // 32) ** -0.5, 0.875, ((0, 8), (1, 4))),
        "latent_projection_bias": gaussian(arg_keys[13], (D,), 0.5, 3.0, ((0, 8),)),
        "prompt_projection_bias": gaussian(arg_keys[14], (D,), 0.5, 3.0, ((0, 8),)),
        "latent_expand": gaussian(arg_keys[15], (D, FF), D ** -0.5, 0.15625, ((0, 8), (1, 4))),
        "prompt_expand": gaussian(arg_keys[16], (D, FF), D ** -0.5, 0.15625, ((0, 8), (1, 4))),
        "latent_expand_bias": gaussian(arg_keys[17], (FF,), 0.5, 3.0, ((0, 4),)),
        "prompt_expand_bias": gaussian(arg_keys[18], (FF,), 0.5, 3.0, ((0, 4),)),
        "latent_contract": gaussian(arg_keys[19], (D, FF), FF ** -0.5, 0.078125, ((0, 8), (1, 4))),
        "prompt_contract": gaussian(arg_keys[20], (D, FF), FF ** -0.5, 0.078125, ((0, 8), (1, 4))),
        "latent_contract_bias": gaussian(arg_keys[21], (D,), 0.5, 3.0, ((0, 8),)),
        "prompt_contract_bias": gaussian(arg_keys[22], (D,), 0.5, 3.0, ((0, 8),)),
        "latent_cotangent": gaussian(arg_keys[23], (SEQS, IMG, D), 1.0, 6.0, ((0, 4), (1, 2))),
        "prompt_cotangent": gaussian(arg_keys[24], (SEQS, TXT, D), 1.0, 6.0, ((0, 4), (1, 2))),
    }


@jax.custom_vjp
def low(v):
    return lax.optimization_barrier(v.astype(jnp.bfloat16)).astype(jnp.float32)

@jax.custom_vjp
def low_back(v):
    return v

def low_keep(v):
    return (low(v), None)

def low_pass(kept, grad):
    return (grad,)

def back_keep(v):
    return (v, None)

def back_low(kept, grad):
    return (low(grad),)
low.defvjp(low_keep, low_pass)
low_back.defvjp(back_keep, back_low)
epsilon = 1e-06
highest = lax.Precision.HIGHEST

def product(form, left, right):
    return jnp.einsum(form, left, right, precision=highest)

def both_ways(values):
    return low(low_back(values))

def normalize(values):
    average = lax.optimization_barrier(jnp.mean(values, axis=-1, keepdims=True))
    centered = values - average
    variance = lax.optimization_barrier(jnp.mean(centered * centered, axis=-1, keepdims=True))
    return centered * lax.rsqrt(variance + epsilon)

def head_attention(head_items):
    queries, key_rows, value_rows = head_items
    scores = low_back(product('qd,kd->qk', queries, key_rows) * HD ** (-0.5))
    weights = jax.nn.softmax(scores, axis=-1)
    return product('qk,kd->qd', low(weights), value_rows)

def stream_in(tokens, modulation, attend, attend_bias):
    shifted = low(normalize(tokens) * (1.0 + modulation[1]) + modulation[0])
    triple = product('td,dkc->ktc', shifted, attend)
    zero_row = jnp.zeros((1, attend_bias.shape[1]), jnp.float32)
    offsets = jnp.concatenate([attend_bias[0:1], zero_row, attend_bias[1:2]], axis=0)
    return both_ways(triple + offsets[:, None, :])

def stream_out(tokens, attended, modulation, project, project_bias, expand, expand_bias, contract, contract_bias):
    projected = low_back(product('td,ed->te', attended, project) + project_bias)
    middle = tokens + modulation[2] * projected
    shifted = low(normalize(middle) * (1.0 + modulation[4]) + modulation[3])
    upward = low_back(product('td,df->tf', shifted, expand) + expand_bias)
    hidden = low(jax.nn.gelu(upward, approximate=True))
    mixed_rows = low_back(product('tf,ef->te', hidden, contract) + contract_bias)
    return middle + modulation[5] * mixed_rows

def forward(latent, prompt, condition, params):
    active = low(jax.nn.silu(condition))
    latent_mod = product('d,dkc->kc', active, params[0]) + params[2]
    prompt_mod = product('d,dkc->kc', active, params[1]) + params[3]
    joined = jnp.concatenate([stream_in(latent, latent_mod, params[4], params[6]), stream_in(prompt, prompt_mod, params[5], params[7])], axis=1)
    length = joined.shape[1]
    by_head = joined.reshape(3, length, HEADS, HD).transpose(0, 2, 1, 3)
    attended = lax.map(jax.checkpoint(head_attention), (by_head[0], by_head[1], by_head[2]))
    attended = both_ways(attended.transpose(1, 0, 2).reshape(length, HEADS * HD))
    latent_out = stream_out(latent, attended[:IMG], latent_mod, params[8], params[10], params[12], params[14], params[16], params[18])
    prompt_out = stream_out(prompt, attended[IMG:], prompt_mod, params[9], params[11], params[13], params[15], params[17], params[19])
    return (latent_out, prompt_out)

def reference(latent_tokens, prompt_tokens, conditioning, latent_modulation, prompt_modulation, latent_modulation_bias, prompt_modulation_bias, latent_attention, prompt_attention, latent_attention_bias, prompt_attention_bias, latent_projection, prompt_projection, latent_projection_bias, prompt_projection_bias, latent_expand, prompt_expand, latent_expand_bias, prompt_expand_bias, latent_contract, prompt_contract, latent_contract_bias, prompt_contract_bias, latent_cotangent, prompt_cotangent):
    raw = (latent_modulation, prompt_modulation, latent_modulation_bias, prompt_modulation_bias, latent_attention, prompt_attention, latent_attention_bias, prompt_attention_bias, latent_projection, prompt_projection, latent_projection_bias, prompt_projection_bias, latent_expand, prompt_expand, latent_expand_bias, prompt_expand_bias, latent_contract, prompt_contract, latent_contract_bias, prompt_contract_bias)
    params = tuple((item.astype(jnp.float32) for item in raw))

    def one_sequence(totals, sequence_items):
        latent, prompt, condition, latent_cot, prompt_cot = sequence_items
        outputs, pullback = jax.vjp(forward, latent.astype(jnp.float32), prompt.astype(jnp.float32), condition.astype(jnp.float32), params)
        grad_latent, grad_prompt, grad_condition, grad_params = pullback((latent_cot.astype(jnp.float32), prompt_cot.astype(jnp.float32)))
        totals = jax.tree.map(jnp.add, totals, grad_params)
        return (totals, (outputs[0].astype(jnp.bfloat16), outputs[1].astype(jnp.bfloat16), grad_latent, grad_prompt, grad_condition))
    zeros = tuple((jnp.zeros(item.shape, jnp.float32) for item in params))
    totals, stacked = lax.scan(one_sequence, zeros, (latent_tokens, prompt_tokens, conditioning, latent_cotangent, prompt_cotangent))
    return (stacked[0], stacked[1], stacked[2], stacked[3], stacked[4], totals[0], totals[1], totals[2], totals[3], totals[4], totals[5], totals[6], totals[7], totals[8], totals[9], totals[10], totals[11], totals[12], totals[13], totals[14], totals[15], totals[16], totals[17], totals[18], totals[19])
```

```python
import jax
import jax.numpy as jnp
from jax import lax
from jax.sharding import PartitionSpec as P

HD = 64


epsilon = 1e-06
highest = lax.Precision.HIGHEST


def normalize(values):
    average = jnp.mean(values, axis=-1, keepdims=True)
    centered = values - average
    variance = jnp.mean(centered * centered, axis=-1, keepdims=True)
    inverse = lax.rsqrt(variance + epsilon)
    return (centered * inverse, inverse)


def normalize_back(upstream, normed, inverse):
    first_mean = jnp.mean(upstream, axis=-1, keepdims=True)
    second_mean = jnp.mean(upstream * normed, axis=-1, keepdims=True)
    return inverse * (upstream - first_mean - normed * second_mean)


def gelu_tanh(values):
    return jax.nn.gelu(values, approximate=True)


def split_heads(blocks):
    seqs_here, length, columns = blocks.shape
    per_seq = columns // HD
    return (
        blocks.reshape(seqs_here, length, per_seq, HD)
        .transpose(0, 2, 1, 3)
        .reshape(seqs_here * per_seq, length, HD)
    )


def merge_heads(blocks, seqs_here):
    per_seq = blocks.shape[0] // seqs_here
    length = blocks.shape[1]
    return (
        blocks.reshape(seqs_here, per_seq, length, HD)
        .transpose(0, 2, 1, 3)
        .reshape(seqs_here, length, per_seq * HD)
    )


def head_forward(head_items):
    queries, key_rows, value_rows = head_items
    factor = HD ** (-0.5)
    scores = jnp.dot(queries, key_rows.T, preferred_element_type=jnp.float32) * factor
    highest_score = jnp.max(scores, axis=-1, keepdims=True)
    exponent = jnp.exp(scores - highest_score)
    totals = jnp.sum(exponent, axis=-1, keepdims=True)
    weights_low = (exponent / totals).astype(jnp.bfloat16)
    attended = jnp.dot(weights_low, value_rows, preferred_element_type=jnp.float32)
    return (attended.astype(jnp.bfloat16), (highest_score + jnp.log(totals))[:, 0])


def head_backward(head_items):
    queries, key_rows, value_rows, logsum, upstream = head_items
    factor = HD ** (-0.5)
    scores = jnp.dot(queries, key_rows.T, preferred_element_type=jnp.float32) * factor
    weights = jnp.exp(scores - logsum[:, None])
    prob_grads = jnp.dot(upstream, value_rows.T, preferred_element_type=jnp.float32)
    score_grads = (
        weights * (prob_grads - jnp.sum(weights * prob_grads, axis=-1, keepdims=True))
    ).astype(jnp.bfloat16)
    query_grads = jnp.dot(score_grads, key_rows, preferred_element_type=jnp.float32) * factor
    key_grads = jnp.dot(score_grads.T, queries, preferred_element_type=jnp.float32) * factor
    value_grads = jnp.dot(
        weights.astype(jnp.bfloat16).T, upstream, preferred_element_type=jnp.float32
    )
    return (
        query_grads.astype(jnp.bfloat16),
        key_grads.astype(jnp.bfloat16),
        value_grads.astype(jnp.bfloat16),
    )


def fetch_weights(shards):
    return (
        lax.all_gather(shards[0], ("fsdp", "heads"), axis=0, tiled=True),
        lax.all_gather(shards[1], ("fsdp", "heads"), axis=0, tiled=True),
        lax.all_gather(shards[2], ("fsdp", "heads"), axis=0, tiled=True),
        lax.all_gather(shards[3], ("fsdp", "heads"), axis=0, tiled=True),
        lax.all_gather(shards[4], ("fsdp", "heads"), axis=0, tiled=True),
        lax.all_gather(shards[5], ("fsdp", "heads"), axis=0, tiled=True),
        lax.all_gather(shards[6], ("fsdp", "heads"), axis=0, tiled=True),
        lax.all_gather(shards[7], ("fsdp", "heads"), axis=0, tiled=True),
        lax.all_gather(shards[8], ("fsdp", "heads"), axis=0, tiled=True),
        lax.all_gather(shards[9], ("fsdp", "heads"), axis=0, tiled=True),
        lax.all_gather(shards[10], ("fsdp", "heads"), axis=0, tiled=True),
        lax.all_gather(shards[11], ("fsdp", "heads"), axis=0, tiled=True),
    )


def weight_row_start(rows_here):
    return (lax.axis_index("fsdp") * lax.axis_size("heads") + lax.axis_index("heads")) * rows_here


def modulate(active, mod_weights, mod_biases):
    everyone = lax.all_gather(active, "fsdp", axis=0, tiled=True)
    rows_here = mod_weights[0].shape[0]
    local_active = lax.dynamic_slice_in_dim(everyone, weight_row_start(rows_here), rows_here, 1)
    latent_part = jnp.einsum(
        "sd,dkc->skc", local_active, mod_weights[0], preferred_element_type=jnp.float32
    )
    prompt_part = jnp.einsum(
        "sd,dkc->skc", local_active, mod_weights[1], preferred_element_type=jnp.float32
    )
    totals = lax.psum((latent_part, prompt_part), ("fsdp", "heads"))
    seqs_here = active.shape[0]
    seq_start = lax.axis_index("fsdp") * seqs_here
    own_latent = (
        lax.dynamic_slice_in_dim(totals[0], seq_start, seqs_here, 0)
        + mod_biases[0].astype(jnp.float32)[None]
    )
    own_prompt = (
        lax.dynamic_slice_in_dim(totals[1], seq_start, seqs_here, 0)
        + mod_biases[1].astype(jnp.float32)[None]
    )
    modulation = (
        lax.all_gather(own_latent, "tensor", axis=2, tiled=True),
        lax.all_gather(own_prompt, "tensor", axis=2, tiled=True),
    )
    return (modulation, local_active)


def tensor_total(partials):
    summed = lax.psum(
        (partials[0].astype(jnp.bfloat16), partials[1].astype(jnp.bfloat16)), "tensor"
    )
    return (summed[0].astype(jnp.float32), summed[1].astype(jnp.float32))


def tensor_grad_total(partials):
    return tensor_total(partials)


def scatter_total(partial):
    reduced = lax.psum_scatter(
        partial.astype(jnp.bfloat16), ("fsdp", "heads"), scatter_dimension=0, tiled=True
    )
    return reduced.astype(jnp.float32)


def forward(streams, modulation, gathered, attend_bias, expand_bias):
    firsts = []
    triples = []
    for stream_index in range(2):
        normed, inverse = normalize(streams[stream_index])
        shifts = modulation[stream_index]
        shifted = (normed * (1.0 + shifts[:, 1:2]) + shifts[:, 0:1]).astype(jnp.bfloat16)
        triple = jnp.einsum(
            "std,dkc->kstc", shifted, gathered[stream_index], preferred_element_type=jnp.float32
        )
        bias_rows = attend_bias[stream_index].astype(jnp.float32)
        offsets = jnp.stack([bias_rows[0], jnp.zeros_like(bias_rows[0]), bias_rows[1]], axis=0)
        triples.append((triple + offsets[:, None, None, :]).astype(jnp.bfloat16))
        firsts.append((normed, inverse, shifted))
    split_at = streams[0].shape[1]
    spread = lax.all_to_all(
        jnp.concatenate(triples, axis=2), "heads", split_axis=3, concat_axis=2, tiled=True
    )
    seqs_here = spread.shape[1]
    heads_in = (split_heads(spread[0]), split_heads(spread[1]), split_heads(spread[2]))
    attended, logsum = lax.map(head_forward, heads_in)
    returned = lax.all_to_all(
        merge_heads(attended, seqs_here), "heads", split_axis=1, concat_axis=2, tiled=True
    )
    attended_rows = (returned[:, :split_at], returned[:, split_at:])
    summed = tensor_total(
        [
            jnp.einsum(
                "std,ed->ste",
                attended_rows[stream_index],
                gathered[2 + stream_index],
                preferred_element_type=jnp.float32,
            )
            for stream_index in range(2)
        ]
    )
    projected = [
        summed[stream_index] + gathered[4 + stream_index].astype(jnp.float32)
        for stream_index in range(2)
    ]
    seconds = []
    mix_parts = []
    for stream_index in range(2):
        shifts = modulation[stream_index]
        middle = streams[stream_index] + shifts[:, 2:3] * projected[stream_index]
        normed, inverse = normalize(middle)
        shifted = (normed * (1.0 + shifts[:, 4:5]) + shifts[:, 3:4]).astype(jnp.bfloat16)
        upward = jnp.einsum(
            "std,df->stf", shifted, gathered[6 + stream_index], preferred_element_type=jnp.float32
        ) + expand_bias[stream_index].astype(jnp.float32)
        hidden = gelu_tanh(upward).astype(jnp.bfloat16)
        mix_parts.append(
            jnp.einsum(
                "stf,ef->ste",
                hidden,
                gathered[8 + stream_index],
                preferred_element_type=jnp.float32,
            )
        )
        seconds.append((middle, normed, inverse, shifted, upward, hidden))
    mix_summed = tensor_total(mix_parts)
    mixed_rows = [
        mix_summed[stream_index] + gathered[10 + stream_index].astype(jnp.float32)
        for stream_index in range(2)
    ]
    results = [
        seconds[stream_index][0] + modulation[stream_index][:, 5:6] * mixed_rows[stream_index]
        for stream_index in range(2)
    ]
    return {
        "firsts": firsts,
        "heads": heads_in,
        "logsum": logsum,
        "attended": attended_rows,
        "projected": projected,
        "seconds": seconds,
        "mixed": mixed_rows,
        "results": results,
    }


def body(
    latent_tokens,
    prompt_tokens,
    conditioning,
    latent_modulation,
    prompt_modulation,
    latent_modulation_bias,
    prompt_modulation_bias,
    latent_attention,
    prompt_attention,
    latent_attention_bias,
    prompt_attention_bias,
    latent_projection,
    prompt_projection,
    latent_projection_bias,
    prompt_projection_bias,
    latent_expand,
    prompt_expand,
    latent_expand_bias,
    prompt_expand_bias,
    latent_contract,
    prompt_contract,
    latent_contract_bias,
    prompt_contract_bias,
    latent_cotangent,
    prompt_cotangent,
):
    shards = (
        latent_attention,
        prompt_attention,
        latent_projection,
        prompt_projection,
        latent_projection_bias,
        prompt_projection_bias,
        latent_expand,
        prompt_expand,
        latent_contract,
        prompt_contract,
        latent_contract_bias,
        prompt_contract_bias,
    )
    attend_bias = (latent_attention_bias, prompt_attention_bias)
    expand_bias = (latent_expand_bias, prompt_expand_bias)
    mod_weights = (latent_modulation, prompt_modulation)
    gathered = fetch_weights(shards)
    cond_full = conditioning.astype(jnp.float32)
    active = jax.nn.silu(cond_full).astype(jnp.bfloat16)
    modulation, local_active = modulate(
        active, mod_weights, (latent_modulation_bias, prompt_modulation_bias)
    )
    streams = (latent_tokens.astype(jnp.float32), prompt_tokens.astype(jnp.float32))
    stored = forward(streams, modulation, gathered, attend_bias, expand_bias)
    latent_result = stored["results"][0].astype(jnp.bfloat16)
    prompt_result = stored["results"][1].astype(jnp.bfloat16)
    weights_back = gathered
    stored_back = stored
    cotangents = (latent_cotangent.astype(jnp.float32), prompt_cotangent.astype(jnp.float32))
    grads = {}
    bias_parts = {}
    statistics = {}
    upward_parts = []
    for stream_index in range(2):
        middle, normed, inverse, shifted, upward, hidden = stored_back["seconds"][stream_index]
        shifts = modulation[stream_index]
        upstream = cotangents[stream_index]
        gate_two = jnp.sum(upstream * stored_back["mixed"][stream_index], axis=1)
        dmixed = (upstream * shifts[:, 5:6]).astype(jnp.bfloat16)
        dhidden = jnp.einsum(
            "ste,ef->stf",
            dmixed,
            weights_back[8 + stream_index],
            preferred_element_type=jnp.float32,
        )
        dupward = jax.vjp(gelu_tanh, upward)[1](dhidden)[0].astype(jnp.bfloat16)
        grads[8 + stream_index] = jnp.einsum(
            "ste,stf->ef", dmixed, hidden, preferred_element_type=jnp.float32
        )
        grads[10 + stream_index] = jnp.sum(dmixed, axis=(0, 1), dtype=jnp.float32)
        grads[6 + stream_index] = jnp.einsum(
            "std,stf->df", shifted, dupward, preferred_element_type=jnp.float32
        )
        bias_parts[2 + stream_index] = jnp.sum(dupward, axis=(0, 1), dtype=jnp.float32)
        upward_parts.append(
            jnp.einsum(
                "stf,df->std",
                dupward,
                weights_back[6 + stream_index],
                preferred_element_type=jnp.float32,
            )
        )
        statistics[stream_index] = gate_two
    dsecond = tensor_grad_total(upward_parts)
    middle_grads = []
    project_parts = []
    for stream_index in range(2):
        middle, normed, inverse, shifted, upward, hidden = stored_back["seconds"][stream_index]
        shifts = modulation[stream_index]
        upstream = dsecond[stream_index]
        shift_two = jnp.sum(upstream, axis=1)
        scale_two = jnp.sum(upstream * normed, axis=1)
        dmiddle = cotangents[stream_index] + normalize_back(
            upstream * (1.0 + shifts[:, 4:5]), normed, inverse
        )
        gate_one = jnp.sum(dmiddle * stored_back["projected"][stream_index], axis=1)
        dproject = (dmiddle * shifts[:, 2:3]).astype(jnp.bfloat16)
        grads[2 + stream_index] = jnp.einsum(
            "ste,std->ed",
            dproject,
            stored_back["attended"][stream_index],
            preferred_element_type=jnp.float32,
        )
        grads[4 + stream_index] = jnp.sum(dproject, axis=(0, 1), dtype=jnp.float32)
        dattended = jnp.einsum(
            "ste,ed->std",
            dproject,
            weights_back[2 + stream_index],
            preferred_element_type=jnp.float32,
        )
        project_parts.append(dattended.astype(jnp.bfloat16))
        middle_grads.append(dmiddle)
        statistics[stream_index] = (gate_one, shift_two, scale_two, statistics[stream_index])
    heads_grad = lax.all_to_all(
        jnp.concatenate(project_parts, axis=1), "heads", split_axis=2, concat_axis=1, tiled=True
    )
    seqs_here = heads_grad.shape[0]
    heads_in = stored_back["heads"]
    query_grads, key_grads, value_grads = lax.map(
        head_backward,
        (heads_in[0], heads_in[1], heads_in[2], stored_back["logsum"], split_heads(heads_grad)),
    )
    stacked = jnp.stack(
        [
            merge_heads(query_grads, seqs_here),
            merge_heads(key_grads, seqs_here),
            merge_heads(value_grads, seqs_here),
        ],
        axis=0,
    )
    returned = lax.all_to_all(stacked, "heads", split_axis=2, concat_axis=3, tiled=True)
    split_at = latent_tokens.shape[1]
    triple_grads = (returned[:, :, :split_at], returned[:, :, split_at:])
    first_parts = []
    for stream_index in range(2):
        normed, inverse, shifted = stored_back["firsts"][stream_index]
        grads[stream_index] = jnp.einsum(
            "std,kstc->dkc", shifted, triple_grads[stream_index], preferred_element_type=jnp.float32
        )
        bias_parts[stream_index] = jnp.sum(
            triple_grads[stream_index], axis=(1, 2), dtype=jnp.float32
        )[::2]
        first_parts.append(
            jnp.einsum(
                "kstc,dkc->std",
                triple_grads[stream_index],
                weights_back[stream_index],
                preferred_element_type=jnp.float32,
            )
        )
    dfirst = tensor_grad_total(first_parts)
    tensor_cols = mod_weights[0].shape[2]
    col_start = lax.axis_index("tensor") * tensor_cols
    token_grads = []
    own_mods = []
    for stream_index in range(2):
        normed, inverse, shifted = stored_back["firsts"][stream_index]
        shifts = modulation[stream_index]
        upstream = dfirst[stream_index]
        token_grads.append(
            middle_grads[stream_index]
            + normalize_back(upstream * (1.0 + shifts[:, 1:2]), normed, inverse)
        )
        gate_one, shift_two, scale_two, gate_two = statistics[stream_index]
        dmodulation = jnp.stack(
            [
                jnp.sum(upstream, axis=1),
                jnp.sum(upstream * normed, axis=1),
                gate_one,
                shift_two,
                scale_two,
                gate_two,
            ],
            axis=1,
        )
        own_mods.append(lax.dynamic_slice_in_dim(dmodulation, col_start, tensor_cols, 2))
    pieces = (
        lax.all_gather(own_mods[0], ("fsdp", "heads"), axis=0, tiled=True),
        lax.all_gather(own_mods[1], ("fsdp", "heads"), axis=0, tiled=True),
    )
    fsdp_count = lax.axis_size("fsdp")
    heads_count = lax.axis_size("heads")
    tensor_count = lax.axis_size("tensor")
    total_seqs = fsdp_count * seqs_here
    rows_here = mod_weights[0].shape[0]
    active_rows_wide = local_active.astype(jnp.float32)
    row_term = jnp.zeros((total_seqs, rows_here), jnp.float32)
    mod_grads = []
    mod_bias_grads = []
    for stream_index in range(2):
        every_mod = pieces[stream_index].reshape(fsdp_count, heads_count, seqs_here, 6, tensor_cols)
        every_mod = jnp.sum(every_mod, axis=1).reshape(total_seqs, 6, tensor_cols)
        mod_grads.append(jnp.einsum("sd,skc->dkc", active_rows_wide, every_mod, precision=highest))
        mod_bias_grads.append(jnp.sum(every_mod, axis=0))
        row_term = row_term + jnp.einsum(
            "skc,dkc->sd",
            every_mod,
            mod_weights[stream_index].astype(jnp.float32),
            precision=highest,
        )
    everywhere = lax.all_gather(row_term[None], ("fsdp", "heads", "tensor"), axis=0, tiled=True)
    folded = jnp.sum(
        everywhere.reshape(fsdp_count * heads_count, tensor_count, total_seqs, rows_here), axis=1
    )
    dactive_all = folded.transpose(1, 0, 2).reshape(
        total_seqs, fsdp_count * heads_count * rows_here
    )
    dactive = lax.dynamic_slice_in_dim(
        dactive_all, lax.axis_index("fsdp") * seqs_here, seqs_here, 0
    )
    conditioning_gradient = jax.vjp(jax.nn.silu, cond_full)[1](dactive)[0]
    bias_totals = lax.psum(
        (bias_parts[0], bias_parts[1], bias_parts[2], bias_parts[3]), ("fsdp", "heads")
    )
    reduced = (
        scatter_total(grads[0]),
        scatter_total(grads[1]),
        scatter_total(grads[2]),
        scatter_total(grads[3]),
        scatter_total(grads[4]),
        scatter_total(grads[5]),
        scatter_total(grads[6]),
        scatter_total(grads[7]),
        scatter_total(grads[8]),
        scatter_total(grads[9]),
        scatter_total(grads[10]),
        scatter_total(grads[11]),
    )
    return (
        latent_result,
        prompt_result,
        token_grads[0],
        token_grads[1],
        conditioning_gradient,
        mod_grads[0],
        mod_grads[1],
        mod_bias_grads[0],
        mod_bias_grads[1],
        reduced[0],
        reduced[1],
        bias_totals[0],
        bias_totals[1],
        reduced[2],
        reduced[3],
        reduced[4],
        reduced[5],
        reduced[6],
        reduced[7],
        bias_totals[2],
        bias_totals[3],
        reduced[8],
        reduced[9],
        reduced[10],
        reduced[11],
    )


def solution(mesh):
    in_specs = (
        P("fsdp", "heads", None),
        P("fsdp", "heads", None),
        P("fsdp", None),
        P(("fsdp", "heads"), None, "tensor"),
        P(("fsdp", "heads"), None, "tensor"),
        P(None, "tensor"),
        P(None, "tensor"),
        P(("fsdp", "heads"), None, "tensor"),
        P(("fsdp", "heads"), None, "tensor"),
        P(None, "tensor"),
        P(None, "tensor"),
        P(("fsdp", "heads"), "tensor"),
        P(("fsdp", "heads"), "tensor"),
        P(("fsdp", "heads")),
        P(("fsdp", "heads")),
        P(("fsdp", "heads"), "tensor"),
        P(("fsdp", "heads"), "tensor"),
        P("tensor"),
        P("tensor"),
        P(("fsdp", "heads"), "tensor"),
        P(("fsdp", "heads"), "tensor"),
        P(("fsdp", "heads")),
        P(("fsdp", "heads")),
        P("fsdp", "heads", None),
        P("fsdp", "heads", None),
    )
    out_specs = (
        P("fsdp", "heads", None),
        P("fsdp", "heads", None),
        P("fsdp", "heads", None),
        P("fsdp", "heads", None),
        P("fsdp", None),
        P(("fsdp", "heads"), None, "tensor"),
        P(("fsdp", "heads"), None, "tensor"),
        P(None, "tensor"),
        P(None, "tensor"),
        P(("fsdp", "heads"), None, "tensor"),
        P(("fsdp", "heads"), None, "tensor"),
        P(None, "tensor"),
        P(None, "tensor"),
        P(("fsdp", "heads"), "tensor"),
        P(("fsdp", "heads"), "tensor"),
        P(("fsdp", "heads")),
        P(("fsdp", "heads")),
        P(("fsdp", "heads"), "tensor"),
        P(("fsdp", "heads"), "tensor"),
        P("tensor"),
        P("tensor"),
        P(("fsdp", "heads"), "tensor"),
        P(("fsdp", "heads"), "tensor"),
        P(("fsdp", "heads")),
        P(("fsdp", "heads")),
    )
    return jax.shard_map(body, mesh=mesh, in_specs=in_specs, out_specs=out_specs, check_vma=False)
```

```python
import functools

import jax
import jax.numpy as jnp
from jax import lax
from jax.experimental import pallas as pl
from jax.experimental.pallas import tpu as pltpu
from jax.sharding import PartitionSpec as P

HD = 64
FSDP, HEADS, TENSOR = "fsdp", "heads", "tensor"
PLANE = (FSDP, HEADS)
EVERY = (FSDP, HEADS, TENSOR)
STEP = 32
SKEW = 4
MESH_ID = pl.DeviceIdType.MESH
f32 = jnp.float32
bf16 = jnp.bfloat16
epsilon = 1e-06
highest = lax.Precision.HIGHEST


def normalize(values):
    average = jnp.mean(values, axis=-1, keepdims=True)
    centered = values - average
    variance = jnp.mean(centered * centered, axis=-1, keepdims=True)
    inverse = lax.rsqrt(variance + epsilon)
    return (centered * inverse, inverse)


def normalize_back(upstream, normed, inverse):
    first_mean = jnp.mean(upstream, axis=-1, keepdims=True)
    second_mean = jnp.mean(upstream * normed, axis=-1, keepdims=True)
    return inverse * (upstream - first_mean - normed * second_mean)


def gelu_tanh(values):
    return jax.nn.gelu(values, approximate=True)


def contract(a, b, left, right):
    return lax.dot_general(a, b, (((left,), (right,)), ((), ())), preferred_element_type=f32)


def flat(values):
    return values.reshape(-1, values.shape[-1])


def rounded_up(count, unit):
    return -(-count // unit) * unit


def group_index(axes):
    index = 0
    for name in axes:
        index = index * lax.axis_size(name) + lax.axis_index(name)
    return index


def group_coords(axes, sizes, index):
    coords = {}
    for name, size in reversed(list(zip(axes, sizes))):
        coords[name] = lax.rem(index, size)
        index = index // size
    return coords


def exchange_kernel(axes, sizes, scatter, source, out, send_sems, recv_sems, own_sem):
    total = 1
    for size in sizes:
        total = total * size
    me = 0
    for name, size in zip(axes, sizes):
        me = me * size + lax.axis_index(name)
    barrier = pltpu.get_barrier_semaphore()

    def greet(k, carry):
        peer = lax.rem(me + k, total)
        pl.semaphore_signal(
            barrier, inc=1, device_id=group_coords(axes, sizes, peer), device_id_type=MESH_ID
        )
        return carry

    lax.fori_loop(1, total, greet, 0)
    own = pltpu.make_async_copy(source.at[me if scatter else 0], out.at[me], own_sem)
    own.start()
    pl.semaphore_wait(barrier, total - 1)

    def copy_to(k):
        peer = lax.rem(me + k, total)
        return pltpu.make_async_remote_copy(
            src_ref=source.at[peer if scatter else 0],
            dst_ref=out.at[me],
            send_sem=send_sems.at[k],
            recv_sem=recv_sems.at[k],
            device_id=group_coords(axes, sizes, peer),
            device_id_type=MESH_ID,
        )

    def send(k, carry):
        copy_to(k).start()
        return carry

    lax.fori_loop(1, total, send, 0)

    def receive(k, carry):
        copy_to(k).wait()
        return carry

    lax.fori_loop(1, total, receive, 0)
    own.wait()


def exchange(values, axes, ident, scatter=False):
    sizes = tuple(lax.axis_size(name) for name in axes)
    total = 1
    for size in sizes:
        total = total * size
    block = values.shape[1:]
    vmem = pl.BlockSpec(memory_space=pltpu.VMEM)
    return pl.pallas_call(
        functools.partial(exchange_kernel, axes, sizes, scatter),
        out_shape=jax.ShapeDtypeStruct((total,) + block, values.dtype),
        in_specs=[vmem],
        out_specs=vmem,
        scratch_shapes=[
            pltpu.SemaphoreType.DMA((total,)),
            pltpu.SemaphoreType.DMA((total,)),
            pltpu.SemaphoreType.DMA,
        ],
        compiler_params=pltpu.CompilerParams(collective_id=ident, has_side_effects=True),
    )(values)


def rows_of_lanes(vector):
    length = vector.shape[0]
    padded = rounded_up(length, 1024)
    return jnp.pad(vector, (0, padded - length)).reshape(padded // 128, 128)


def total_kernel(n, offsets, a0, a1, w_all, out, w0, w1, w_sems, part, land_up, land_down, s_up, r_up, s_down, r_down, bs_up, br_up, bs_down, br_down):
    rows0 = a0.shape[0]
    rows1 = a1.shape[0]
    width = w0.shape[0]
    half = width // 2
    block = 256 if rows0 % 256 == 0 else rows0
    tiles = width // 256
    step = STEP
    per_block = block // step
    count = (rows0 + rows1) // step
    main = rows0 // step
    d = lax.axis_index(TENSOR)

    def tile0(b, t):
        rows = pl.ds(pl.multiple_of(b * block, block), block)
        cols = pl.ds(pl.multiple_of(t * 256, 256), 256)
        part[rows, cols] = contract(a0[rows, :], w0[cols, :], 1, 1).astype(bf16)

    def tile1(t):
        cols = pl.ds(pl.multiple_of(t * 256, 256), 256)
        part[pl.ds(rows0, rows1), cols] = contract(a1[...], w1[cols, :], 1, 1).astype(bf16)

    def rows_of(i):
        return pl.ds(pl.multiple_of(i * step, step), step)

    up_cols = pl.ds(0, half)
    down_cols = pl.ds(half, half)

    def reduce_copy(up, i):
        cols, land, ss, rs = (up_cols, land_up, s_up, r_up) if up else (down_cols, land_down, s_down, r_down)
        return pltpu.make_async_remote_copy(
            src_ref=part.at[rows_of(i), cols],
            dst_ref=land.at[rows_of(i)],
            send_sem=ss.at[i],
            recv_sem=rs.at[i],
            device_id={TENSOR: d + 1 if up else d - 1},
            device_id_type=MESH_ID,
        )

    def spread_copy(up, i):
        cols, ss, rs = (up_cols, bs_up, br_up) if up else (down_cols, bs_down, br_down)
        return pltpu.make_async_remote_copy(
            src_ref=out.at[rows_of(i), cols],
            dst_ref=out.at[rows_of(i), cols],
            send_sem=ss.at[i],
            recv_sem=rs.at[i],
            device_id={TENSOR: d - 1 if up else d + 1},
            device_id_type=MESH_ID,
        )

    def merged(up, i):
        cols, land = (up_cols, land_up) if up else (down_cols, land_down)
        return (part[rows_of(i), cols].astype(f32) + land[rows_of(i), :].astype(f32)).astype(bf16)

    loads = [
        pltpu.make_async_copy(w_all.at[:, pl.ds(offset, w.shape[1])], w, w_sems.at[i])
        for i, (offset, w) in enumerate(zip(offsets, (w0, w1)))
    ]
    for load in loads:
        load.start()
    barrier = pltpu.get_barrier_semaphore()

    @pl.when(d > 0)
    def _():
        pl.semaphore_signal(barrier, inc=1, device_id={TENSOR: d - 1}, device_id_type=MESH_ID)

    @pl.when(d < n - 1)
    def _():
        pl.semaphore_signal(barrier, inc=1, device_id={TENSOR: d + 1}, device_id_type=MESH_ID)

    for load in loads:
        load.wait()
    for t in range(tiles):
        tile0(0, t)

    ends = (d == 0) | (d == n - 1)

    @pl.when(ends)
    def _():
        pl.semaphore_wait(barrier, 1)

    @pl.when(jnp.logical_not(ends))
    def _():
        pl.semaphore_wait(barrier, 2)

    def end_role(up_source):
        def flood(i, _):
            b = i // per_block
            t = lax.rem(i, per_block)

            reduce_copy(up_source, i).start()

            @pl.when((b + 1 < rows0 // block) & (t == 0))
            def _():
                def inner(t2, _):
                    tile0(b + 1, t2)
                    return 0
                lax.fori_loop(0, tiles, inner, 0)
            return 0

        lax.fori_loop(0, main, flood, 0)

        def tail_tile(t, _):
            tile1(t)
            return 0

        lax.fori_loop(0, tiles, tail_tile, 0)

        def flood_tail(i, _):
            reduce_copy(up_source, i).start()
            return 0

        lax.fori_loop(main, count, flood_tail, 0)

        def finish(i, _):
            other = not up_source
            reduce_copy(other, i).wait_recv()
            cols = up_cols if other else down_cols
            out[rows_of(i), cols] = merged(other, i)
            spread_copy(other, i).start()
            return 0

        lax.fori_loop(0, count, finish, 0)

        def gather(i, _):
            spread_copy(up_source, i).wait_recv()
            reduce_copy(up_source, i).wait_send()
            spread_copy(not up_source, i).wait_send()
            return 0

        lax.fori_loop(0, count, gather, 0)

    @pl.when(d == 0)
    def _():
        end_role(True)

    @pl.when(d == n - 1)
    def _():
        end_role(False)

    @pl.when((d > 0) & (d < n - 1))
    def _():
        def relay(up, i):
            cols = up_cols if up else down_cols
            reduce_copy(up, i).wait_recv()
            part[rows_of(i), cols] = merged(up, i)
            reduce_copy(up, i).start()

        lag = SKEW * (n - 3)
        late_up = SKEW * (d - 1)
        late_down = SKEW * (n - 2 - d)

        def within(i):
            return (i >= 0) & (i < count)

        def pass_on(t, _):
            for up, late in ((True, late_up), (False, late_down)):
                i = t - late

                @pl.when(within(i))
                def _():
                    relay(up, i)

            b = t // per_block
            tile = lax.rem(t, per_block)

            @pl.when((b + 1 < rows0 // block) & (tile < tiles))
            def _():
                tile0(b + 1, tile)

            @pl.when((b + 1 == rows0 // block) & (tile < tiles))
            def _():
                tile1(tile)
            return 0

        lax.fori_loop(0, count + lag, pass_on, 0)

        def spread(t, _):
            for up, late in ((True, late_down), (False, late_up)):
                i = t - late

                @pl.when(within(i))
                def _():
                    spread_copy(up, i).wait_recv()
                    spread_copy(up, i).start()
            return 0

        lax.fori_loop(0, count + lag, spread, 0)

        def drain(i, _):
            for up in (True, False):
                reduce_copy(up, i).wait_send()
                spread_copy(up, i).wait_send()
            return 0

        lax.fori_loop(0, count, drain, 0)


def matmul_total(a0, a1, w_all, offsets, ident):
    n = lax.axis_size(TENSOR)
    rows = a0.shape[0] + a1.shape[0]
    width = w_all.shape[0]
    count = rows // STEP
    depth = a0.shape[1]
    dma = pltpu.SemaphoreType.DMA((count,))
    vmem = pl.BlockSpec(memory_space=pltpu.VMEM)
    return pl.pallas_call(
        functools.partial(total_kernel, n, offsets),
        out_shape=jax.ShapeDtypeStruct((rows, width), bf16),
        in_specs=[vmem, vmem, pl.BlockSpec(memory_space=pl.ANY)],
        out_specs=vmem,
        scratch_shapes=[
            pltpu.VMEM((width, depth), bf16),
            pltpu.VMEM((width, depth), bf16),
            pltpu.SemaphoreType.DMA((2,)),
            pltpu.VMEM((rows, width), bf16),
            pltpu.VMEM((rows, width // 2), bf16),
            pltpu.VMEM((rows, width // 2), bf16),
        ]
        + [dma] * 8,
        compiler_params=pltpu.CompilerParams(
            collective_id=ident, has_side_effects=True, vmem_limit_bytes=56000000
        ),
        cost_estimate=pl.CostEstimate(
            flops=2 * rows * width * a0.shape[1], bytes_accessed=300 * 10**6, transcendentals=0
        ),
    )(a0, a1, w_all)


def query_blocks(main, padded):
    unit = 256 if main % 256 == 0 else 128
    spans = [(start, unit) for start in range(0, main, unit)]
    return spans + [(main, padded - main)]


def key_bias(main, text, valid):
    half = main + text
    row = lax.broadcasted_iota(jnp.int32, (2 * half, 1), 0)
    inside = jnp.where(row >= half, row - half, row)
    return jnp.where(inside >= main + valid, -1e30, 0.0).astype(f32)


def gather_rows(target, pieces):
    start = 0
    for piece in pieces:
        target[pl.ds(start, piece.shape[1]), :] = piece[0]
        start += piece.shape[1]
    return start


def stack_queries(target, main, text, factor):
    lead, tail = main.shape[1], text.shape[1]
    target[pl.ds(0, lead), :] = main[0] * factor
    target[pl.ds(lead, tail), :] = text[0] * factor
    rest = target.shape[0] - lead - tail
    target[pl.ds(lead + tail, rest), :] = jnp.zeros((rest, target.shape[1]), target.dtype)


def attend_kernel(valid, qi, qt, ki, kt, ji, jt, vi, vt, ui, ut, oi, ot, li, lt, q_all, k_all, v_all, o_all):
    main, text = qi.shape[1], qt.shape[1]
    stack_queries(q_all, qi, qt, jnp.asarray(HD**-0.5, bf16))
    gather_rows(k_all, (ki, kt, ji, jt))
    gather_rows(v_all, (vi, vt, ui, ut))
    bias = key_bias(main, text, valid)
    lane = lax.broadcasted_iota(jnp.int32, (1, 2 * HD), 1)
    for head in range(2):
        mine = (lane >= head * HD) & (lane < (head + 1) * HD)
        for start, size in query_blocks(main, q_all.shape[0]):
            queries = jnp.where(mine, q_all[pl.ds(start, size), :], jnp.zeros((), bf16))
            scores = contract(k_all[...], queries, 1, 1) + bias
            top = jnp.max(scores, axis=0, keepdims=True)
            exponent = jnp.exp(scores - top)
            total = jnp.sum(exponent, axis=0, keepdims=True)
            weights = (exponent * (1.0 / total)).astype(bf16)
            attended = contract(v_all[...], weights, 0, 0)
            o_all[pl.ds(head * HD, HD), pl.ds(start, size)] = attended[head * HD : (head + 1) * HD]
            logsum = top + jnp.log(total)
            if start < main:
                li[0, 0, pl.ds(head, 1), pl.ds(start, size)] = logsum
            else:
                lt[0, 0, pl.ds(head, 1), :] = logsum
    joined = o_all[...].T.astype(bf16)
    oi[0] = joined[:main]
    ot[0] = joined[main : main + text]


def attend_back_kernel(
    valid, qi, qt, ki, kt, ji, jt, vi, vt, ui, ut, gi, gt, li, lt,
    dqi, dqt, dki, dkt, dji, djt, dvi, dvt, dui, dut,
    q_all, k_all, v_all, g_all, dq_all, dk_all, dv_all,
):
    main, text = qi.shape[1], qt.shape[1]
    stack_queries(q_all, qi, qt, jnp.asarray(HD**-0.5, bf16))
    stack_queries(g_all, gi, gt, jnp.asarray(1.0, bf16))
    gather_rows(k_all, (ki, kt, ji, jt))
    gather_rows(v_all, (vi, vt, ui, ut))
    bias = key_bias(main, text, valid)
    lane = lax.broadcasted_iota(jnp.int32, (1, 2 * HD), 1)
    first = True
    for head in range(2):
        mine = (lane >= head * HD) & (lane < (head + 1) * HD)
        for start, size in query_blocks(main, q_all.shape[0]):
            queries = jnp.where(mine, q_all[pl.ds(start, size), :], jnp.zeros((), bf16))
            upstream = jnp.where(mine, g_all[pl.ds(start, size), :], jnp.zeros((), bf16))
            if start < main:
                logsum = li[0, 0, pl.ds(head, 1), pl.ds(start, size)]
            else:
                logsum = lt[0, 0, pl.ds(head, 1), :]
            weights = jnp.exp(contract(k_all[...], queries, 1, 1) + bias - logsum)
            prob_grads = contract(v_all[...], upstream, 1, 1)
            row_sum = jnp.sum(weights * prob_grads, axis=0, keepdims=True)
            score_grads = (weights * (prob_grads - row_sum)).astype(bf16)
            key_part = contract(score_grads, queries, 1, 0)
            value_part = contract(weights.astype(bf16), upstream, 1, 0)
            if first:
                dk_all[...] = key_part
                dv_all[...] = value_part
            else:
                dk_all[...] += key_part
                dv_all[...] += value_part
            first = False
            query_part = contract(k_all[...], score_grads, 0, 0)
            dq_all[pl.ds(head * HD, HD), pl.ds(start, size)] = query_part[head * HD : (head + 1) * HD]
    joined = (dq_all[...].T * HD**-0.5).astype(bf16)
    dqi[0] = joined[:main]
    dqt[0] = joined[main : main + text]
    for source, targets in ((dk_all, (dki, dkt, dji, djt)), (dv_all, (dvi, dvt, dui, dut))):
        start = 0
        for target in targets:
            rows = target.shape[1]
            target[0] = source[pl.ds(start, rows), :].astype(bf16)
            start += rows


def head_block(rows, offset):
    return pl.BlockSpec((1, rows, 2 * HD), lambda s, p: (s, 0, p + offset))


def attention_call(kernel, shapes, operands, in_offsets, outputs, scratch, cost):
    seqs, pairs = shapes
    in_specs = []
    for operand, offset in zip(operands, in_offsets):
        if operand.ndim == 4:
            in_specs.append(pl.BlockSpec((1, 1) + operand.shape[2:], lambda s, p: (s, p, 0, 0)))
        else:
            in_specs.append(head_block(operand.shape[1], offset))
    out_specs = []
    for output in outputs:
        if len(output.shape) == 4:
            out_specs.append(pl.BlockSpec((1, 1) + output.shape[2:], lambda s, p: (s, p, 0, 0)))
        else:
            out_specs.append(head_block(output.shape[1], 0))
    return pl.pallas_call(
        kernel,
        grid=(seqs, pairs),
        out_shape=outputs,
        in_specs=in_specs,
        out_specs=out_specs,
        scratch_shapes=scratch,
        compiler_params=pltpu.CompilerParams(vmem_limit_bytes=56000000),
        cost_estimate=cost,
    )(*operands)


def attend(q, kv, far, valid):
    seqs, main, columns = q[0].shape
    text = q[1].shape[1]
    pairs = columns // (2 * HD)
    padded = main + rounded_up(text, 128)
    keys = 2 * (main + text)
    operands = (q[0], q[1], kv[0], kv[1], far[0], far[1], kv[0], kv[1], far[0], far[1])
    offsets = (0, 0, 0, 0, 0, 0, pairs, pairs, pairs, pairs)
    outputs = (
        jax.ShapeDtypeStruct((seqs, main, columns), bf16),
        jax.ShapeDtypeStruct((seqs, text, columns), bf16),
        jax.ShapeDtypeStruct((seqs, pairs, 2, main), f32),
        jax.ShapeDtypeStruct((seqs, pairs, 2, padded - main), f32),
    )
    wide = 2 * HD
    scratch = [
        pltpu.VMEM((padded, wide), bf16),
        pltpu.VMEM((keys, wide), bf16),
        pltpu.VMEM((keys, wide), bf16),
        pltpu.VMEM((wide, padded), f32),
    ]
    cost = pl.CostEstimate(
        flops=2 * 4 * seqs * pairs * padded * keys * wide, bytes_accessed=10**7,
        transcendentals=2 * seqs * pairs * padded * keys,
    )
    return attention_call(
        functools.partial(attend_kernel, valid), (seqs, pairs), operands, offsets, outputs, scratch, cost
    )


def attend_back(q, kv, far, upstream, logsums, valid):
    seqs, main, columns = q[0].shape
    text = q[1].shape[1]
    pairs = columns // (2 * HD)
    padded = main + rounded_up(text, 128)
    keys = 2 * (main + text)
    operands = (q[0], q[1], kv[0], kv[1], far[0], far[1], kv[0], kv[1], far[0], far[1]) + (
        upstream[0], upstream[1], logsums[0], logsums[1],
    )
    offsets = (0, 0, 0, 0, 0, 0, pairs, pairs, pairs, pairs, 0, 0, 0, 0)
    image_shape = jax.ShapeDtypeStruct((seqs, main, columns), bf16)
    text_shape = jax.ShapeDtypeStruct((seqs, text, columns), bf16)
    outputs = (image_shape, text_shape) * 5
    wide = 2 * HD
    scratch = [
        pltpu.VMEM((padded, wide), bf16),
        pltpu.VMEM((keys, wide), bf16),
        pltpu.VMEM((keys, wide), bf16),
        pltpu.VMEM((padded, wide), bf16),
        pltpu.VMEM((wide, padded), f32),
        pltpu.VMEM((keys, wide), f32),
        pltpu.VMEM((keys, wide), f32),
    ]
    cost = pl.CostEstimate(
        flops=10**6, bytes_accessed=10**6, transcendentals=0
    )
    return attention_call(
        functools.partial(attend_back_kernel, valid), (seqs, pairs), operands, offsets, outputs, scratch, cost
    )


def gathered_rows(shards):
    return lax.all_gather(jnp.concatenate(shards, axis=1), PLANE, axis=0, tiled=True)


def scatter_total(partials):
    partial = jnp.concatenate(partials, axis=1)
    return lax.psum_scatter(partial, PLANE, scatter_dimension=0, tiled=True)


def cut(values, like):
    pieces, start = [], 0
    for item in like:
        pieces.append(values[:, start : start + item.shape[1]].astype(f32))
        start += item.shape[1]
    return pieces


def swap_halves(values):
    count = lax.axis_size(HEADS)
    pairs = [(i, count - 1 - i) for i in range(count)]
    return lax.ppermute(values, HEADS, pairs)


def low_product(a, b, left, right):
    return contract(a, b, left, right).astype(bf16)


def body(
    latent_tokens, prompt_tokens, conditioning,
    latent_modulation, prompt_modulation, latent_modulation_bias, prompt_modulation_bias,
    latent_attention, prompt_attention, latent_attention_bias, prompt_attention_bias,
    latent_projection, prompt_projection, latent_projection_bias, prompt_projection_bias,
    latent_expand, prompt_expand, latent_expand_bias, prompt_expand_bias,
    latent_contract, prompt_contract, latent_contract_bias, prompt_contract_bias,
    latent_cotangent, prompt_cotangent,
):
    both = range(2)
    fsdp_count, heads_count = lax.axis_size(FSDP), lax.axis_size(HEADS)
    tensor_count = lax.axis_size(TENSOR)
    plane_count = fsdp_count * heads_count
    seqs, text, width = prompt_tokens.shape
    rows_here = latent_projection.shape[0]
    columns = latent_projection.shape[1]
    all_seqs = seqs * fsdp_count
    padded_text = rounded_up(seqs * text, STEP) // seqs
    while (padded_text * seqs) % STEP or padded_text % 16:
        padded_text += 1
    pad_text = ((0, 0), (0, padded_text - text), (0, 0))
    tokens = (latent_tokens, jnp.pad(prompt_tokens, pad_text))
    cotangents = (latent_cotangent, jnp.pad(prompt_cotangent, pad_text))
    mod_weights = (latent_modulation, prompt_modulation)
    attend_bias = (latent_attention_bias, prompt_attention_bias)
    expand_bias = (latent_expand_bias, prompt_expand_bias)

    third = 3 * columns
    hidden_here = latent_expand.shape[1]
    attend_all = gathered_rows(
        [latent_attention.reshape(rows_here, third), prompt_attention.reshape(rows_here, third)]
    )
    project_all = gathered_rows([latent_projection, prompt_projection])
    w_attend = [attend_all[:, i * third : (i + 1) * third] for i in both]
    w_project = [project_all[:, i * columns : (i + 1) * columns] for i in both]

    cond_full = conditioning.astype(f32)
    active = jax.nn.silu(cond_full).astype(bf16).astype(f32)
    biases = jnp.concatenate(
        [latent_projection_bias, prompt_projection_bias, latent_contract_bias, prompt_contract_bias]
    ).astype(f32)
    packed = rows_of_lanes(jnp.concatenate([active.reshape(-1), biases]))
    spread = exchange(packed[None], PLANE, 1).reshape(plane_count, -1)
    everyone = spread[:, : seqs * width].reshape(fsdp_count, heads_count, seqs, width)[:, 0]
    everyone = everyone.reshape(all_seqs, width)
    biases = spread[:, seqs * width : seqs * width + 4 * rows_here].reshape(plane_count, 4, rows_here)
    biases = biases.transpose(1, 0, 2).reshape(4, width)
    project_bias, contract_bias = biases[:2], biases[2:]

    own_row = group_index(PLANE) * rows_here
    local_active = lax.dynamic_slice_in_dim(everyone, own_row, rows_here, 1)
    active_low = local_active.astype(bf16)
    parts = jnp.stack([contract(active_low, w, 1, 0) for w in mod_weights])
    parts = parts.reshape(2, fsdp_count, seqs, 6, columns).transpose(1, 0, 2, 3, 4)
    parts = parts.reshape(fsdp_count, 1, -1, 128)
    parts = jnp.broadcast_to(parts, (fsdp_count, heads_count) + parts.shape[2:])
    parts = exchange(parts.reshape((plane_count,) + parts.shape[2:]), PLANE, 2, scatter=True)
    own_mod = jnp.sum(parts, axis=0).reshape(2, seqs, 6, columns)
    mod_bias = jnp.stack([latent_modulation_bias, prompt_modulation_bias]).astype(f32)
    own_mod = (own_mod + mod_bias[:, None]).reshape(1, -1, 128)
    modulation = exchange(own_mod, (TENSOR,), 3).reshape(tensor_count, 2, seqs, 6, columns)
    modulation = modulation.transpose(1, 2, 3, 0, 4).reshape(2, seqs, 6, 1, width)

    firsts, queries, pairs_kv = [], [], []
    for i in both:
        normed, inverse = normalize(tokens[i].astype(f32))
        shifted = (normed * (1.0 + modulation[i, :, 1]) + modulation[i, :, 0]).astype(bf16)
        firsts.append((normed, inverse, flat(shifted)))
    for i in both:
        bias = attend_bias[i].astype(f32)
        kv_bias = jnp.concatenate([jnp.zeros_like(bias[1]), bias[1]])
        kv = contract(firsts[i][2], w_attend[i][:, columns:], 1, 0) + kv_bias
        pairs_kv.append(kv.astype(bf16).reshape(seqs, -1, 2 * columns))
        query = contract(firsts[i][2], w_attend[i][:, :columns], 1, 0) + bias[0]
        queries.append(query.astype(bf16).reshape(seqs, -1, columns))
    far_kv = [swap_halves(kv) for kv in pairs_kv]
    wide_shards = [latent_expand, prompt_expand, latent_contract, prompt_contract]
    far_kv, wide_shards = lax.optimization_barrier((far_kv, wide_shards))
    wide_all = gathered_rows(wide_shards)
    w_wide = [wide_all[:, i * hidden_here : (i + 1) * hidden_here] for i in range(4)]
    w_expand, w_contract = w_wide[:2], w_wide[2:]
    attended_image, attended_text, *logsums = attend(queries, pairs_kv, far_kv, text)
    attended = (flat(attended_image), flat(attended_text))
    split = attended[0].shape[0]

    def streams(total):
        return [
            total[:split].reshape(seqs, -1, width).astype(f32),
            total[split:].reshape(seqs, -1, width).astype(f32),
        ]

    projected = streams(matmul_total(
        attended[0], attended[1], project_all, (0, columns), 4
    ))
    projected = [projected[i] + project_bias[i] for i in both]

    seconds, mix_parts = [], []
    for i in both:
        middle = tokens[i].astype(f32) + modulation[i, :, 2] * projected[i]
        normed, inverse = normalize(middle)
        shifted = flat((normed * (1.0 + modulation[i, :, 4]) + modulation[i, :, 3]).astype(bf16))
        upward = contract(shifted, w_expand[i], 1, 0) + expand_bias[i].astype(f32)
        hidden = gelu_tanh(upward).astype(bf16)
        seconds.append((middle, normed, inverse, shifted, upward, hidden))
    for i in both:
        mix_parts.append(low_product(seconds[i][5], w_contract[i], 1, 1))

    grads, bias_parts, upward_grads = {}, {}, []
    for i in both:
        upward, hidden = seconds[i][4:]
        upstream = cotangents[i].astype(f32)
        dmixed = flat((upstream * modulation[i, :, 5]).astype(bf16))
        dhidden = contract(dmixed, w_contract[i], 1, 0)
        dupward = jax.vjp(gelu_tanh, upward)[1](dhidden)[0].astype(bf16)
        upward_grads.append(dupward)
        grads[i + 6] = low_product(dmixed, hidden, 0, 0)
        bias_parts[i + 2] = jnp.sum(dmixed, axis=0, dtype=f32)
        bias_parts[i + 6] = jnp.sum(dupward, axis=0, dtype=f32)
    upward_grads, grads[6], grads[7] = lax.optimization_barrier(
        (upward_grads, grads[6], grads[7])
    )
    dsecond = matmul_total(upward_grads[0], upward_grads[1], wide_all, (0, hidden_here), 5)
    reduced = [scatter_total([grads[6], grads[7]])]
    dsecond, mix_parts, reduced = lax.optimization_barrier((dsecond, mix_parts, reduced))
    dsecond = streams(dsecond)
    mixed = lax.psum_scatter(
        jnp.concatenate(mix_parts), TENSOR, scatter_dimension=0, tiled=True
    )

    statistics, middle_grads, attended_grads, project_grads = [], [], [], []
    for i in both:
        middle, normed, inverse = seconds[i][:3]
        shifts = modulation[i]
        upstream = dsecond[i]
        dmiddle = cotangents[i].astype(f32) + normalize_back(
            upstream * (1.0 + shifts[:, 4]), normed, inverse
        )
        dproject = flat((dmiddle * shifts[:, 2]).astype(bf16))
        attended_grads.append(
            low_product(dproject, w_project[i], 1, 0).reshape(seqs, -1, columns)
        )
        statistics.append(
            [
                jnp.sum(dmiddle * projected[i], axis=1),
                jnp.sum(upstream, axis=1),
                jnp.sum(upstream * normed, axis=1),
            ]
        )
        project_grads.append(dproject)
        bias_parts[i] = jnp.sum(dproject, axis=0, dtype=f32)
        middle_grads.append(dmiddle)

    back = attend_back(queries, pairs_kv, far_kv, attended_grads, logsums, text)
    back, upward_grads, project_grads, mixed = lax.optimization_barrier(
        (back, upward_grads, project_grads, mixed)
    )
    mixed = lax.all_gather(mixed, TENSOR, axis=0, tiled=True)
    for i in both:
        grads[i + 4] = low_product(seconds[i][3], upward_grads[i], 0, 0)
        grads[i + 2] = low_product(project_grads[i], attended[i], 0, 0)
    far_grads = [swap_halves(jnp.concatenate([back[4 + i], back[8 + i]], axis=2)) for i in both]
    far_grads, grads = lax.optimization_barrier((far_grads, grads))
    triple_grads = []
    for i in both:
        own = jnp.concatenate([back[2 + i], back[6 + i]], axis=2).astype(f32)
        pair = (own + far_grads[i].astype(f32)).astype(bf16)
        triple_grads.append(flat(jnp.concatenate([back[i], pair], axis=2)))
    for i in both:
        grads[i] = low_product(firsts[i][2], triple_grads[i], 0, 0)
        bias_parts[i + 4] = jnp.sum(triple_grads[i], axis=0, dtype=f32)
    triple_grads, grads, mixed = lax.optimization_barrier((triple_grads, grads, mixed))
    dfirst = matmul_total(triple_grads[0], triple_grads[1], attend_all, (0, third), 6)
    reduced.append(scatter_total([grads[i] for i in (4, 5, 2, 3)]))
    dfirst, reduced, mixed, grads = lax.optimization_barrier((dfirst, reduced, mixed, grads))
    mixed = streams(mixed)
    reduced.append(scatter_total([grads[0], grads[1]]))
    dfirst = streams(dfirst)

    results = []
    for i in both:
        mixed_rows = mixed[i] + contract_bias[i]
        results.append((seconds[i][0] + modulation[i, :, 5] * mixed_rows).astype(bf16))
        statistics[i].append(jnp.sum(cotangents[i].astype(f32) * mixed_rows, axis=1))

    token_grads, own_mods = [], []
    column_start = lax.axis_index(TENSOR) * columns
    for i in both:
        normed, inverse, _ = firsts[i]
        upstream = dfirst[i]
        token_grads.append(
            middle_grads[i]
            + normalize_back(upstream * (1.0 + modulation[i, :, 1]), normed, inverse)
        )
        gate_one, shift_two, scale_two, gate_two = statistics[i]
        dmodulation = jnp.stack(
            [
                jnp.sum(upstream, axis=1),
                jnp.sum(upstream * normed, axis=1),
                gate_one,
                shift_two,
                scale_two,
                gate_two,
            ],
            axis=1,
        )
        own_mods.append(lax.dynamic_slice_in_dim(dmodulation, column_start, columns, 2))
    own_mods = jnp.stack(own_mods).reshape(-1, 128)
    mod_rows = own_mods.shape[0]
    packed = rows_of_lanes(jnp.concatenate([bias_parts[i] for i in range(8)]))
    pieces = exchange(jnp.concatenate([own_mods, packed])[None], PLANE, 8)
    bias_totals = jnp.sum(pieces[:, mod_rows:], axis=0).reshape(-1)
    bias_grads, start = [], 0
    for i in range(8):
        length = bias_parts[i].shape[0]
        bias_grads.append(bias_totals[start : start + length])
        start += length
    own_bias = [lax.dynamic_slice_in_dim(bias_grads[i], own_row, rows_here, 0) for i in range(4)]
    attend_bias_grads = [bias_grads[i].reshape(3, columns)[::2] for i in (4, 5)]
    pieces = pieces[:, :mod_rows].reshape(fsdp_count, heads_count, 2, seqs, 6, columns).sum(axis=1)
    every_mod = pieces.transpose(1, 0, 2, 3, 4).reshape(2, all_seqs, 6, columns)
    row_term = jnp.zeros((all_seqs, rows_here), f32)
    mod_grads, mod_bias_grads = [], []
    for i in both:
        mod_grads.append(
            jnp.einsum("sd,skc->dkc", local_active, every_mod[i], precision=highest)
        )
        mod_bias_grads.append(jnp.sum(every_mod[i], axis=0))
        row_term = row_term + jnp.einsum(
            "skc,dkc->sd", every_mod[i], mod_weights[i].astype(f32), precision=highest
        )
    term_length = seqs * rows_here
    row_term = row_term.reshape(fsdp_count, term_length)
    row_term = jnp.pad(row_term, ((0, 0), (0, rounded_up(term_length, 1024) - term_length)))
    copies = heads_count * tensor_count
    row_term = row_term.reshape(fsdp_count, 1, -1, 128)
    row_term = jnp.broadcast_to(row_term, (fsdp_count, copies) + row_term.shape[2:])
    terms = exchange(row_term.reshape((fsdp_count * copies,) + row_term.shape[2:]), EVERY, 9, scatter=True)
    terms = terms.reshape(plane_count, tensor_count, -1)[:, :, :term_length].sum(axis=1)
    dactive = terms.reshape(plane_count, seqs, rows_here).transpose(1, 0, 2).reshape(seqs, width)
    conditioning_gradient = jax.vjp(jax.nn.silu, cond_full)[1](dactive)[0]

    order = ((6, 7), (4, 5, 2, 3), (0, 1))
    reduced = [cut(item, [grads[i] for i in keys]) for item, keys in zip(reduced, order)]
    reduced = {i: part for parts, keys in zip(reduced, order) for i, part in zip(keys, parts)}
    shape = latent_attention.shape
    return (
        results[0], results[1][:, :text], token_grads[0], token_grads[1][:, :text],
        conditioning_gradient,
        mod_grads[0], mod_grads[1], mod_bias_grads[0], mod_bias_grads[1],
        reduced[0].reshape(shape), reduced[1].reshape(shape),
        attend_bias_grads[0], attend_bias_grads[1],
        reduced[2], reduced[3], own_bias[0], own_bias[1],
        reduced[4], reduced[5], bias_grads[6], bias_grads[7],
        reduced[6], reduced[7], own_bias[2], own_bias[3],
    )


def solution(mesh):
    rows, tens = P(FSDP, HEADS, None), P(None, TENSOR)
    wide, flat2, line = P(PLANE, None, TENSOR), P(PLANE, TENSOR), P(PLANE)
    hid = P(TENSOR)
    weights = (
        wide, wide, tens, tens, wide, wide, tens, tens, flat2, flat2, line, line,
        flat2, flat2, hid, hid, flat2, flat2, line, line,
    )
    cond = P(FSDP, None)
    in_specs = (rows, rows, cond) + weights + (rows, rows)
    out_specs = (rows, rows, rows, rows, cond) + weights
    return jax.shard_map(body, mesh=mesh, in_specs=in_specs, out_specs=out_specs, check_vma=False)
```

```python
import functools

import jax
import jax.numpy as jnp
from jax import lax
from jax.experimental import pallas as pl
from jax.experimental.pallas import tpu as pltpu
from jax.sharding import PartitionSpec as P

HD = 64
FSDP, HEADS, TENSOR = "fsdp", "heads", "tensor"
PLANE = (FSDP, HEADS)
EVERY = (FSDP, HEADS, TENSOR)
STEP = 32
SKEW = 4
MESH_ID = pl.DeviceIdType.MESH
f32 = jnp.float32
bf16 = jnp.bfloat16
epsilon = 1e-06
highest = lax.Precision.HIGHEST


def normalize(values):
    average = jnp.mean(values, axis=-1, keepdims=True)
    centered = values - average
    variance = jnp.mean(centered * centered, axis=-1, keepdims=True)
    inverse = lax.rsqrt(variance + epsilon)
    return (centered * inverse, inverse)


def normalize_back(upstream, normed, inverse):
    first_mean = jnp.mean(upstream, axis=-1, keepdims=True)
    second_mean = jnp.mean(upstream * normed, axis=-1, keepdims=True)
    return inverse * (upstream - first_mean - normed * second_mean)


def gelu_tanh(values):
    return jax.nn.gelu(values, approximate=True)


def contract(a, b, left, right):
    return lax.dot_general(a, b, (((left,), (right,)), ((), ())), preferred_element_type=f32)


def flat(values):
    return values.reshape(-1, values.shape[-1])


def rounded_up(count, unit):
    return -(-count // unit) * unit


def group_index(axes):
    index = 0
    for name in axes:
        index = index * lax.axis_size(name) + lax.axis_index(name)
    return index


def group_coords(axes, sizes, index):
    coords = {}
    for name, size in reversed(list(zip(axes, sizes))):
        coords[name] = lax.rem(index, size)
        index = index // size
    return coords


def exchange_kernel(axes, sizes, scatter, source, out, send_sems, recv_sems, own_sem):
    total = 1
    for size in sizes:
        total = total * size
    me = 0
    for name, size in zip(axes, sizes):
        me = me * size + lax.axis_index(name)
    barrier = pltpu.get_barrier_semaphore()

    def greet(k, carry):
        peer = lax.rem(me + k, total)
        pl.semaphore_signal(
            barrier, inc=1, device_id=group_coords(axes, sizes, peer), device_id_type=MESH_ID
        )
        return carry

    lax.fori_loop(1, total, greet, 0)
    own = pltpu.make_async_copy(source.at[me if scatter else 0], out.at[me], own_sem)
    own.start()
    pl.semaphore_wait(barrier, total - 1)

    def copy_to(k):
        peer = lax.rem(me + k, total)
        return pltpu.make_async_remote_copy(
            src_ref=source.at[peer if scatter else 0],
            dst_ref=out.at[me],
            send_sem=send_sems.at[k],
            recv_sem=recv_sems.at[k],
            device_id=group_coords(axes, sizes, peer),
            device_id_type=MESH_ID,
        )

    def send(k, carry):
        copy_to(k).start()
        return carry

    lax.fori_loop(1, total, send, 0)

    def receive(k, carry):
        copy_to(k).wait()
        return carry

    lax.fori_loop(1, total, receive, 0)
    own.wait()


def exchange(values, axes, ident, scatter=False):
    sizes = tuple(lax.axis_size(name) for name in axes)
    total = 1
    for size in sizes:
        total = total * size
    block = values.shape[1:]
    vmem = pl.BlockSpec(memory_space=pltpu.VMEM)
    return pl.pallas_call(
        functools.partial(exchange_kernel, axes, sizes, scatter),
        out_shape=jax.ShapeDtypeStruct((total,) + block, values.dtype),
        in_specs=[vmem],
        out_specs=vmem,
        scratch_shapes=[
            pltpu.SemaphoreType.DMA((total,)),
            pltpu.SemaphoreType.DMA((total,)),
            pltpu.SemaphoreType.DMA,
        ],
        compiler_params=pltpu.CompilerParams(collective_id=ident, has_side_effects=True),
        cost_estimate=pl.CostEstimate(flops=1, bytes_accessed=1024, transcendentals=0),
    )(values)


def rows_of_lanes(vector):
    length = vector.shape[0]
    padded = rounded_up(length, 1024)
    return jnp.pad(vector, (0, padded - length)).reshape(padded // 128, 128)


def total_kernel(n, offsets, a0, a1, w_all, out, w0, w1, w_sems, part, land_up, land_down, s_up, r_up, s_down, r_down, bs_up, br_up, bs_down, br_down):
    rows0 = a0.shape[0]
    rows1 = a1.shape[0]
    width = w0.shape[0]
    half = width // 2
    block = 256 if rows0 % 256 == 0 else rows0
    tiles = width // 256
    step = STEP
    per_block = block // step
    count = (rows0 + rows1) // step
    main = rows0 // step
    d = lax.axis_index(TENSOR)

    def tile0(b, t):
        rows = pl.ds(pl.multiple_of(b * block, block), block)
        cols = pl.ds(pl.multiple_of(t * 256, 256), 256)
        part[rows, cols] = contract(a0[rows, :], w0[cols, :], 1, 1).astype(bf16)

    def tile1(t):
        cols = pl.ds(pl.multiple_of(t * 256, 256), 256)
        part[pl.ds(rows0, rows1), cols] = contract(a1[...], w1[cols, :], 1, 1).astype(bf16)

    def rows_of(i):
        return pl.ds(pl.multiple_of(i * step, step), step)

    up_cols = pl.ds(0, half)
    down_cols = pl.ds(half, half)

    def reduce_copy(up, i):
        cols, land, ss, rs = (up_cols, land_up, s_up, r_up) if up else (down_cols, land_down, s_down, r_down)
        return pltpu.make_async_remote_copy(
            src_ref=part.at[rows_of(i), cols],
            dst_ref=land.at[rows_of(i)],
            send_sem=ss.at[i],
            recv_sem=rs.at[i],
            device_id={TENSOR: d + 1 if up else d - 1},
            device_id_type=MESH_ID,
        )

    def spread_copy(up, i):
        cols, ss, rs = (up_cols, bs_up, br_up) if up else (down_cols, bs_down, br_down)
        return pltpu.make_async_remote_copy(
            src_ref=out.at[rows_of(i), cols],
            dst_ref=out.at[rows_of(i), cols],
            send_sem=ss.at[i],
            recv_sem=rs.at[i],
            device_id={TENSOR: d - 1 if up else d + 1},
            device_id_type=MESH_ID,
        )

    def merged(up, i):
        cols, land = (up_cols, land_up) if up else (down_cols, land_down)
        return (part[rows_of(i), cols].astype(f32) + land[rows_of(i), :].astype(f32)).astype(bf16)

    loads = [
        pltpu.make_async_copy(w_all.at[:, pl.ds(offset, w.shape[1])], w, w_sems.at[i])
        for i, (offset, w) in enumerate(zip(offsets, (w0, w1)))
    ]
    for load in loads:
        load.start()
    barrier = pltpu.get_barrier_semaphore()

    @pl.when(d > 0)
    def _():
        pl.semaphore_signal(barrier, inc=1, device_id={TENSOR: d - 1}, device_id_type=MESH_ID)

    @pl.when(d < n - 1)
    def _():
        pl.semaphore_signal(barrier, inc=1, device_id={TENSOR: d + 1}, device_id_type=MESH_ID)

    for load in loads:
        load.wait()
    for t in range(tiles):
        tile0(0, t)

    ends = (d == 0) | (d == n - 1)

    @pl.when(ends)
    def _():
        pl.semaphore_wait(barrier, 1)

    @pl.when(jnp.logical_not(ends))
    def _():
        pl.semaphore_wait(barrier, 2)

    def end_role(up_source):
        def flood(i, _):
            b = i // per_block
            t = lax.rem(i, per_block)

            reduce_copy(up_source, i).start()

            @pl.when((b + 1 < rows0 // block) & (t == 0))
            def _():
                def inner(t2, _):
                    tile0(b + 1, t2)
                    return 0
                lax.fori_loop(0, tiles, inner, 0)
            return 0

        lax.fori_loop(0, main, flood, 0)

        def tail_tile(t, _):
            tile1(t)
            return 0

        lax.fori_loop(0, tiles, tail_tile, 0)

        def flood_tail(i, _):
            reduce_copy(up_source, i).start()
            return 0

        lax.fori_loop(main, count, flood_tail, 0)

        def finish(i, _):
            other = not up_source
            reduce_copy(other, i).wait_recv()
            cols = up_cols if other else down_cols
            out[rows_of(i), cols] = merged(other, i)
            spread_copy(other, i).start()
            return 0

        lax.fori_loop(0, count, finish, 0)

        def gather(i, _):
            spread_copy(up_source, i).wait_recv()
            reduce_copy(up_source, i).wait_send()
            spread_copy(not up_source, i).wait_send()
            return 0

        lax.fori_loop(0, count, gather, 0)

    @pl.when(d == 0)
    def _():
        end_role(True)

    @pl.when(d == n - 1)
    def _():
        end_role(False)

    @pl.when((d > 0) & (d < n - 1))
    def _():
        def relay(up, i):
            cols = up_cols if up else down_cols
            reduce_copy(up, i).wait_recv()
            part[rows_of(i), cols] = merged(up, i)
            reduce_copy(up, i).start()

        lag = SKEW * (n - 3)
        late_up = SKEW * (d - 1)
        late_down = SKEW * (n - 2 - d)

        def within(i):
            return (i >= 0) & (i < count)

        def pass_on(t, _):
            for up, late in ((True, late_up), (False, late_down)):
                i = t - late

                @pl.when(within(i))
                def _():
                    relay(up, i)

            b = t // per_block
            tile = lax.rem(t, per_block)

            @pl.when((b + 1 < rows0 // block) & (tile < tiles))
            def _():
                tile0(b + 1, tile)

            @pl.when((b + 1 == rows0 // block) & (tile < tiles))
            def _():
                tile1(tile)
            return 0

        lax.fori_loop(0, count + lag, pass_on, 0)

        def spread(t, _):
            for up, late in ((True, late_down), (False, late_up)):
                i = t - late

                @pl.when(within(i))
                def _():
                    spread_copy(up, i).wait_recv()
                    spread_copy(up, i).start()
            return 0

        lax.fori_loop(0, count + lag, spread, 0)

        def drain(i, _):
            for up in (True, False):
                reduce_copy(up, i).wait_send()
                spread_copy(up, i).wait_send()
            return 0

        lax.fori_loop(0, count, drain, 0)


def matmul_total(a0, a1, w_all, offsets, ident):
    n = lax.axis_size(TENSOR)
    rows = a0.shape[0] + a1.shape[0]
    width = w_all.shape[0]
    count = rows // STEP
    depth = a0.shape[1]
    dma = pltpu.SemaphoreType.DMA((count,))
    vmem = pl.BlockSpec(memory_space=pltpu.VMEM)
    return pl.pallas_call(
        functools.partial(total_kernel, n, offsets),
        out_shape=jax.ShapeDtypeStruct((rows, width), bf16),
        in_specs=[vmem, vmem, pl.BlockSpec(memory_space=pl.ANY)],
        out_specs=vmem,
        scratch_shapes=[
            pltpu.VMEM((width, depth), bf16),
            pltpu.VMEM((width, depth), bf16),
            pltpu.SemaphoreType.DMA((2,)),
            pltpu.VMEM((rows, width), bf16),
            pltpu.VMEM((rows, width // 2), bf16),
            pltpu.VMEM((rows, width // 2), bf16),
        ]
        + [dma] * 8,
        compiler_params=pltpu.CompilerParams(
            collective_id=ident, has_side_effects=True, vmem_limit_bytes=56000000
        ),
        cost_estimate=pl.CostEstimate(
            flops=2 * rows * width * a0.shape[1], bytes_accessed=300 * 10**6, transcendentals=0
        ),
    )(a0, a1, w_all)


def query_blocks(main, padded):
    unit = 256 if main % 256 == 0 else 128
    spans = [(start, unit) for start in range(0, main, unit)]
    return spans + [(main, padded - main)]


def key_bias(main, text, valid):
    half = main + text
    row = lax.broadcasted_iota(jnp.int32, (2 * half, 1), 0)
    inside = jnp.where(row >= half, row - half, row)
    return jnp.where(inside >= main + valid, -1e30, 0.0).astype(f32)


def gather_rows(target, pieces, seq, cols):
    start = 0
    for piece in pieces:
        rows = piece.shape[1]
        target[pl.ds(start, rows), :] = piece[seq, :, cols]
        start += rows


def stack_queries(target, main, text, seq, cols, factor):
    lead, tail = main.shape[1], text.shape[1]
    target[pl.ds(0, lead), :] = main[seq, :, cols] * factor
    target[pl.ds(lead, tail), :] = text[seq, :, cols] * factor
    rest = target.shape[0] - lead - tail
    target[pl.ds(lead + tail, rest), :] = jnp.zeros((rest, target.shape[1]), target.dtype)


def lanes_at(pair, offset):
    return pl.ds(pl.multiple_of(pair * 2 * HD + offset, 2 * HD), 2 * HD)


def meet_partner():
    partner = lax.axis_size(HEADS) - 1 - lax.axis_index(HEADS)
    barrier = pltpu.get_barrier_semaphore()
    pl.semaphore_signal(barrier, inc=1, device_id={HEADS: partner}, device_id_type=MESH_ID)
    pl.semaphore_wait(barrier, 1)
    return partner


def head_lanes(head):
    lane = lax.broadcasted_iota(jnp.int32, (1, 2 * HD), 1)
    return (lane >= head * HD) & (lane < (head + 1) * HD)


def attend_kernel(valid, pairs, ti, tt, oi, ot, li, lt, fi, ft, q_all, k_all, v_all, o_all, sends, receives):
    seqs, main, _ = ti.shape
    text = tt.shape[1]
    columns = pairs * 2 * HD
    partner = meet_partner()

    def copies(t):
        seq, pair = t // pairs, lax.rem(t, pairs)
        made = []
        for source, target in ((ti, fi), (tt, ft)):
            for part in range(2):
                which = len(made)
                made.append(
                    pltpu.make_async_remote_copy(
                        src_ref=source.at[seq, :, lanes_at(pair, columns * (1 + part))],
                        dst_ref=target.at[seq, :, lanes_at(pair, columns * part)],
                        send_sem=sends.at[t, which],
                        recv_sem=receives.at[t, which],
                        device_id={HEADS: partner},
                        device_id_type=MESH_ID,
                    )
                )
        return made

    def send(t, carry):
        for copy in copies(t):
            copy.start()
        return carry

    lax.fori_loop(0, seqs * pairs, send, 0)
    bias = key_bias(main, text, valid)

    def step(t, carry):
        seq, pair = t // pairs, lax.rem(t, pairs)
        stack_queries(q_all, ti, tt, seq, lanes_at(pair, 0), jnp.asarray(HD**-0.5, bf16))
        for copy in copies(t):
            copy.wait_recv()
        half = main + text
        for target, part in ((k_all, 0), (v_all, 1)):
            gather_rows(target.at[pl.ds(0, half)], (ti, tt), seq, lanes_at(pair, columns * (1 + part)))
            gather_rows(target.at[pl.ds(half, half)], (fi, ft), seq, lanes_at(pair, columns * part))
        for head in range(2):
            mine = head_lanes(head)
            for start, size in query_blocks(main, q_all.shape[0]):
                queries = jnp.where(mine, q_all[pl.ds(start, size), :], jnp.zeros((), bf16))
                scores = contract(k_all[...], queries, 1, 1) + bias
                top = jnp.max(scores, axis=0, keepdims=True)
                exponent = jnp.exp(scores - top)
                total = jnp.sum(exponent, axis=0, keepdims=True)
                weights = (exponent * (1.0 / total)).astype(bf16)
                attended = contract(v_all[...], weights, 0, 0)
                o_all[pl.ds(head * HD, HD), pl.ds(start, size)] = attended[head * HD : (head + 1) * HD]
                logsum = top + jnp.log(total)
                if start < main:
                    li[seq, pair, pl.ds(head, 1), pl.ds(start, size)] = logsum
                else:
                    lt[seq, pair, pl.ds(head, 1), :] = logsum
        joined = o_all[...].T.astype(bf16)
        oi[seq, :, lanes_at(pair, 0)] = joined[:main]
        ot[seq, :, lanes_at(pair, 0)] = joined[main : main + text]
        return carry

    lax.fori_loop(0, seqs * pairs, step, 0)

    def finish(t, carry):
        for copy in copies(t):
            copy.wait_send()
        return carry

    lax.fori_loop(0, seqs * pairs, finish, 0)


def attend_back_kernel(
    valid, pairs, ti, tt, fi, ft, gi, gt, li, lt, di, dt,
    q_all, k_all, v_all, g_all, dq_all, dk_all, dv_all, own, away_i, away_t, land_i, land_t, sends, receives,
):
    seqs, main, _ = ti.shape
    text = tt.shape[1]
    half = main + text
    columns = pairs * 2 * HD
    partner = meet_partner()

    def copies(t):
        seq, pair = t // pairs, lax.rem(t, pairs)
        made = []
        for source, target in ((away_i, land_i), (away_t, land_t)):
            for part in range(2):
                which = len(made)
                cols = lanes_at(pair, columns * part)
                made.append(
                    pltpu.make_async_remote_copy(
                        src_ref=source.at[seq, :, cols],
                        dst_ref=target.at[seq, :, cols],
                        send_sem=sends.at[t, which],
                        recv_sem=receives.at[t, which],
                        device_id={HEADS: partner},
                        device_id_type=MESH_ID,
                    )
                )
        return made

    bias = key_bias(main, text, valid)

    def step(t, carry):
        seq, pair = t // pairs, lax.rem(t, pairs)
        stack_queries(q_all, ti, tt, seq, lanes_at(pair, 0), jnp.asarray(HD**-0.5, bf16))
        stack_queries(g_all, gi, gt, seq, lanes_at(pair, 0), jnp.asarray(1.0, bf16))
        for target, part in ((k_all, 0), (v_all, 1)):
            gather_rows(target.at[pl.ds(0, half)], (ti, tt), seq, lanes_at(pair, columns * (1 + part)))
            gather_rows(target.at[pl.ds(half, half)], (fi, ft), seq, lanes_at(pair, columns * part))
        first = True
        for head in range(2):
            mine = head_lanes(head)
            for start, size in query_blocks(main, q_all.shape[0]):
                queries = jnp.where(mine, q_all[pl.ds(start, size), :], jnp.zeros((), bf16))
                upstream = jnp.where(mine, g_all[pl.ds(start, size), :], jnp.zeros((), bf16))
                if start < main:
                    logsum = li[seq, pair, pl.ds(head, 1), pl.ds(start, size)]
                else:
                    logsum = lt[seq, pair, pl.ds(head, 1), :]
                weights = jnp.exp(contract(k_all[...], queries, 1, 1) + bias - logsum)
                prob_grads = contract(v_all[...], upstream, 1, 1)
                row_sum = jnp.sum(weights * prob_grads, axis=0, keepdims=True)
                score_grads = (weights * (prob_grads - row_sum)).astype(bf16)
                key_part = contract(score_grads, queries, 1, 0)
                value_part = contract(weights.astype(bf16), upstream, 1, 0)
                if first:
                    dk_all[...] = key_part
                    dv_all[...] = value_part
                else:
                    dk_all[...] += key_part
                    dv_all[...] += value_part
                first = False
                query_part = contract(k_all[...], score_grads, 0, 0)
                dq_all[pl.ds(head * HD, HD), pl.ds(start, size)] = query_part[
                    head * HD : (head + 1) * HD
                ]
        for part, source in ((0, dk_all), (1, dv_all)):
            cols = lanes_at(pair, columns * part)
            away_i[seq, :, cols] = source[pl.ds(half, main), :].astype(bf16)
            away_t[seq, :, cols] = source[pl.ds(half + main, text), :].astype(bf16)
            own[seq, :, cols] = source[pl.ds(0, half), :]
        joined = (dq_all[...].T * HD**-0.5).astype(bf16)
        di[seq, :, lanes_at(pair, 0)] = joined[:main]
        dt[seq, :, lanes_at(pair, 0)] = joined[main : main + text]
        for copy in copies(t):
            copy.start()
        return carry

    lax.fori_loop(0, seqs * pairs, step, 0)

    def finish(t, carry):
        seq, pair = t // pairs, lax.rem(t, pairs)
        for copy in copies(t):
            copy.wait()
        for part in range(2):
            cols = lanes_at(pair, columns * part)
            out_cols = lanes_at(pair, columns * (1 + part))
            mine = own[seq, :, cols]
            di[seq, :, out_cols] = (mine[:main] + land_i[seq, :, cols].astype(f32)).astype(bf16)
            dt[seq, :, out_cols] = (mine[main:] + land_t[seq, :, cols].astype(f32)).astype(bf16)
        return carry

    lax.fori_loop(0, seqs * pairs, finish, 0)


def attention_call(kernel, operands, outputs, scratch, ident, factor):
    seqs, main, columns = operands[0].shape
    pairs = columns // (6 * HD)
    work = seqs * pairs * main * main * 8 * 2 * HD * factor
    vmem = pl.BlockSpec(memory_space=pltpu.VMEM)
    copies = pltpu.SemaphoreType.DMA((seqs * pairs, 4))
    return pl.pallas_call(
        kernel,
        out_shape=outputs,
        in_specs=[vmem] * len(operands),
        out_specs=[vmem] * len(outputs),
        scratch_shapes=scratch + [copies, copies],
        compiler_params=pltpu.CompilerParams(
            collective_id=ident, has_side_effects=True, vmem_limit_bytes=56000000
        ),
        cost_estimate=pl.CostEstimate(flops=work, bytes_accessed=10**7, transcendentals=0),
    )(*operands)


def attend(triples, valid, ident):
    seqs, main, columns = triples[0].shape
    columns = columns // 3
    text = triples[1].shape[1]
    wide = 2 * HD
    pairs = columns // wide
    padded = main + rounded_up(text, 128)
    keys = 2 * (main + text)
    outputs = (
        jax.ShapeDtypeStruct((seqs, main, columns), bf16),
        jax.ShapeDtypeStruct((seqs, text, columns), bf16),
        jax.ShapeDtypeStruct((seqs, pairs, 2, main), f32),
        jax.ShapeDtypeStruct((seqs, pairs, 2, padded - main), f32),
        jax.ShapeDtypeStruct((seqs, main, 2 * columns), bf16),
        jax.ShapeDtypeStruct((seqs, text, 2 * columns), bf16),
    )
    scratch = [
        pltpu.VMEM((padded, wide), bf16),
        pltpu.VMEM((keys, wide), bf16),
        pltpu.VMEM((keys, wide), bf16),
        pltpu.VMEM((wide, padded), f32),
    ]
    kernel = functools.partial(attend_kernel, valid, pairs)
    return attention_call(kernel, tuple(triples), outputs, scratch, ident, 2)


def attend_back(triples, far, upstream, logsums, valid, ident):
    seqs, main, columns = triples[0].shape
    columns = columns // 3
    text = triples[1].shape[1]
    wide = 2 * HD
    pairs = columns // wide
    padded = main + rounded_up(text, 128)
    keys = 2 * (main + text)
    operands = tuple(triples) + tuple(far) + tuple(upstream) + tuple(logsums)
    outputs = tuple(jax.ShapeDtypeStruct(item.shape, bf16) for item in triples)
    scratch = [
        pltpu.VMEM((padded, wide), bf16),
        pltpu.VMEM((keys, wide), bf16),
        pltpu.VMEM((keys, wide), bf16),
        pltpu.VMEM((padded, wide), bf16),
        pltpu.VMEM((wide, padded), f32),
        pltpu.VMEM((keys, wide), f32),
        pltpu.VMEM((keys, wide), f32),
        pltpu.VMEM((seqs, main + text, 2 * columns), f32),
        pltpu.VMEM((seqs, main, 2 * columns), bf16),
        pltpu.VMEM((seqs, text, 2 * columns), bf16),
        pltpu.VMEM((seqs, main, 2 * columns), bf16),
        pltpu.VMEM((seqs, text, 2 * columns), bf16),
    ]
    kernel = functools.partial(attend_back_kernel, valid, pairs)
    return attention_call(kernel, operands, outputs, scratch, ident, 5)


def gathered_rows(shards):
    return lax.all_gather(jnp.concatenate(shards, axis=1), PLANE, axis=0, tiled=True)


def scatter_total(partials):
    partial = jnp.concatenate(partials, axis=1)
    return lax.psum_scatter(partial, PLANE, scatter_dimension=0, tiled=True)


def gate_gradient(slab, cotangents, seqs, columns, ident):
    count = slab.shape[0]
    start = lax.axis_index(TENSOR) * count
    image_rows, text_rows = (item.shape[0] for item in cotangents)
    upstream = lax.dynamic_slice_in_dim(jnp.concatenate(cotangents), start, count, 0)
    product = upstream.astype(f32) * slab.astype(f32)
    row = start + lax.broadcasted_iota(jnp.int32, (2 * seqs, count), 1)
    group = lax.broadcasted_iota(jnp.int32, (2 * seqs, count), 0)
    per_image, per_text = image_rows // seqs, text_rows // seqs
    text_row = row - image_rows
    place = jnp.where(row < image_rows, row // per_image, seqs + text_row // per_text)
    chosen = (place == group).astype(f32)
    sums = jnp.dot(chosen, product, precision=highest)
    tensor_count = lax.axis_size(TENSOR)
    sums = sums.reshape(2 * seqs, tensor_count, columns).transpose(1, 0, 2)
    length = 2 * seqs * columns
    sums = sums.reshape(tensor_count, length)
    sums = jnp.pad(sums, ((0, 0), (0, rounded_up(length, 1024) - length)))
    sums = exchange(sums.reshape(tensor_count, -1, 128), (TENSOR,), ident, scatter=True)
    return jnp.sum(sums, axis=0).reshape(-1)[:length].reshape(2, seqs, columns)


def cut(values, like):
    pieces, start = [], 0
    for item in like:
        pieces.append(values[:, start : start + item.shape[1]].astype(f32))
        start += item.shape[1]
    return pieces


def low_product(a, b, left, right):
    return contract(a, b, left, right).astype(bf16)


def body(
    latent_tokens, prompt_tokens, conditioning,
    latent_modulation, prompt_modulation, latent_modulation_bias, prompt_modulation_bias,
    latent_attention, prompt_attention, latent_attention_bias, prompt_attention_bias,
    latent_projection, prompt_projection, latent_projection_bias, prompt_projection_bias,
    latent_expand, prompt_expand, latent_expand_bias, prompt_expand_bias,
    latent_contract, prompt_contract, latent_contract_bias, prompt_contract_bias,
    latent_cotangent, prompt_cotangent,
):
    both = range(2)
    fsdp_count, heads_count = lax.axis_size(FSDP), lax.axis_size(HEADS)
    tensor_count = lax.axis_size(TENSOR)
    plane_count = fsdp_count * heads_count
    seqs, text, width = prompt_tokens.shape
    rows_here = latent_projection.shape[0]
    columns = latent_projection.shape[1]
    all_seqs = seqs * fsdp_count
    padded_text = rounded_up(seqs * text, STEP) // seqs
    while (padded_text * seqs) % STEP or padded_text % 16:
        padded_text += 1
    pad_text = ((0, 0), (0, padded_text - text), (0, 0))
    tokens = (latent_tokens, jnp.pad(prompt_tokens, pad_text))
    cotangents = (latent_cotangent, jnp.pad(prompt_cotangent, pad_text))
    mod_weights = (latent_modulation, prompt_modulation)
    attend_bias = (latent_attention_bias, prompt_attention_bias)
    expand_bias = (latent_expand_bias, prompt_expand_bias)

    third = 3 * columns
    hidden_here = latent_expand.shape[1]
    attend_all = gathered_rows(
        [latent_attention.reshape(rows_here, third), prompt_attention.reshape(rows_here, third)]
    )
    w_attend = [attend_all[:, i * third : (i + 1) * third] for i in both]

    cond_full = conditioning.astype(f32)
    active = jax.nn.silu(cond_full).astype(bf16).astype(f32)
    biases = jnp.concatenate(
        [latent_projection_bias, prompt_projection_bias, latent_contract_bias, prompt_contract_bias]
    ).astype(f32)
    packed = rows_of_lanes(jnp.concatenate([active.reshape(-1), biases]))
    spread = exchange(packed[None], PLANE, 1).reshape(plane_count, -1)
    everyone = spread[:, : seqs * width].reshape(fsdp_count, heads_count, seqs, width)[:, 0]
    everyone = everyone.reshape(all_seqs, width)
    biases = spread[:, seqs * width : seqs * width + 4 * rows_here].reshape(plane_count, 4, rows_here)
    biases = biases.transpose(1, 0, 2).reshape(4, width)
    project_bias, contract_bias = biases[:2], biases[2:]

    own_row = group_index(PLANE) * rows_here
    local_active = lax.dynamic_slice_in_dim(everyone, own_row, rows_here, 1)
    active_low = local_active.astype(bf16)
    parts = jnp.stack([contract(active_low, w, 1, 0) for w in mod_weights])
    parts = parts.reshape(2, fsdp_count, seqs, 6, columns).transpose(1, 0, 2, 3, 4)
    parts = parts.reshape(fsdp_count, 1, -1, 128)
    parts = jnp.broadcast_to(parts, (fsdp_count, heads_count) + parts.shape[2:])
    parts = exchange(parts.reshape((plane_count,) + parts.shape[2:]), PLANE, 2, scatter=True)
    own_mod = jnp.sum(parts, axis=0).reshape(2, seqs, 6, columns)
    mod_bias = jnp.stack([latent_modulation_bias, prompt_modulation_bias]).astype(f32)
    own_mod = (own_mod + mod_bias[:, None]).reshape(1, -1, 128)
    modulation = exchange(own_mod, (TENSOR,), 3).reshape(tensor_count, 2, seqs, 6, columns)
    modulation = modulation.transpose(1, 2, 3, 0, 4).reshape(2, seqs, 6, 1, width)

    firsts, triples = [], []
    for i in both:
        normed, inverse = normalize(tokens[i].astype(f32))
        shifted = (normed * (1.0 + modulation[i, :, 1]) + modulation[i, :, 0]).astype(bf16)
        firsts.append((normed, inverse, flat(shifted)))
    for i in both:
        bias = attend_bias[i].astype(f32)
        offsets = jnp.concatenate([bias[0], jnp.zeros_like(bias[0]), bias[1]])
        triple = contract(firsts[i][2], w_attend[i], 1, 0) + offsets
        triples.append(triple.astype(bf16).reshape(seqs, -1, third))
    project_all = gathered_rows([latent_projection, prompt_projection])
    w_project = [project_all[:, i * columns : (i + 1) * columns] for i in both]
    attended_image, attended_text, *logsums, far_image, far_text = attend(triples, text, 10)
    attended_image, attended_text, wide_shards = lax.optimization_barrier(
        (
            attended_image,
            attended_text,
            [latent_expand, prompt_expand, latent_contract, prompt_contract],
        )
    )
    wide_all = gathered_rows(wide_shards)
    w_wide = [wide_all[:, i * hidden_here : (i + 1) * hidden_here] for i in range(4)]
    w_expand, w_contract = w_wide[:2], w_wide[2:]
    attended = (flat(attended_image), flat(attended_text))
    split = attended[0].shape[0]

    def streams(total):
        return [
            total[:split].reshape(seqs, -1, width).astype(f32),
            total[split:].reshape(seqs, -1, width).astype(f32),
        ]

    projected = streams(matmul_total(
        attended[0], attended[1], project_all, (0, columns), 4
    ))
    projected = [projected[i] + project_bias[i] for i in both]

    seconds, mix_parts = [], []
    for i in both:
        middle = tokens[i].astype(f32) + modulation[i, :, 2] * projected[i]
        normed, inverse = normalize(middle)
        shifted = flat((normed * (1.0 + modulation[i, :, 4]) + modulation[i, :, 3]).astype(bf16))
        upward = contract(shifted, w_expand[i], 1, 0) + expand_bias[i].astype(f32)
        hidden = gelu_tanh(upward).astype(bf16)
        seconds.append((middle, normed, inverse, shifted, upward, hidden))
    for i in both:
        mix_parts.append(low_product(seconds[i][5], w_contract[i], 1, 1))

    grads, bias_parts, upward_grads = {}, {}, []
    for i in both:
        upward, hidden = seconds[i][4:]
        upstream = cotangents[i].astype(f32)
        dmixed = flat((upstream * modulation[i, :, 5]).astype(bf16))
        dhidden = contract(dmixed, w_contract[i], 1, 0)
        dupward = jax.vjp(gelu_tanh, upward)[1](dhidden)[0].astype(bf16)
        upward_grads.append(dupward)
        grads[i + 6] = low_product(dmixed, hidden, 0, 0)
        bias_parts[i + 2] = jnp.sum(dmixed, axis=0, dtype=f32)
        bias_parts[i + 6] = jnp.sum(dupward, axis=0, dtype=f32)
    grads[5] = low_product(seconds[1][3], upward_grads[1], 0, 0)
    upward_grads, grads = lax.optimization_barrier((upward_grads, grads))
    dsecond = matmul_total(upward_grads[0], upward_grads[1], wide_all, (0, hidden_here), 5)
    reduced = [scatter_total([grads[i] for i in (6, 7, 5)])]
    dsecond, mix_parts, reduced = lax.optimization_barrier((dsecond, mix_parts, reduced))
    dsecond = streams(dsecond)
    mixed = lax.psum_scatter(
        jnp.concatenate(mix_parts), TENSOR, scatter_dimension=0, tiled=True
    )

    statistics, middle_grads, attended_grads, project_grads = [], [], [], []
    for i in both:
        middle, normed, inverse = seconds[i][:3]
        shifts = modulation[i]
        upstream = dsecond[i]
        dmiddle = cotangents[i].astype(f32) + normalize_back(
            upstream * (1.0 + shifts[:, 4]), normed, inverse
        )
        dproject = flat((dmiddle * shifts[:, 2]).astype(bf16))
        attended_grads.append(
            low_product(dproject, w_project[i], 1, 0).reshape(seqs, -1, columns)
        )
        statistics.append(
            [
                jnp.sum(dmiddle * projected[i], axis=1),
                jnp.sum(upstream, axis=1),
                jnp.sum(upstream * normed, axis=1),
            ]
        )
        project_grads.append(dproject)
        bias_parts[i] = jnp.sum(dproject, axis=0, dtype=f32)
        middle_grads.append(dmiddle)

    for i in both:
        grads[i + 2] = low_product(project_grads[i], attended[i], 0, 0)
    grads[4] = low_product(seconds[0][3], upward_grads[0], 0, 0)
    attended_grads, grads = lax.optimization_barrier((attended_grads, grads))
    reduced.append(scatter_total([grads[i] for i in (4, 2, 3)]))
    back = attend_back(triples, (far_image, far_text), attended_grads, logsums, text, 11)
    back, mixed = lax.optimization_barrier((back, mixed))
    gate_two = gate_gradient(mixed, [flat(item) for item in cotangents], seqs, columns, 7)
    triple_grads = [flat(item) for item in back]
    for i in both:
        grads[i] = low_product(firsts[i][2], triple_grads[i], 0, 0)
        bias_parts[i + 4] = jnp.sum(triple_grads[i], axis=0, dtype=f32)
    triple_grads, grads = lax.optimization_barrier((triple_grads, grads))
    last_reduced = scatter_total([grads[0], grads[1]])
    dfirst = matmul_total(triple_grads[0], triple_grads[1], attend_all, (0, third), 6)
    dfirst, reduced, mixed = lax.optimization_barrier((dfirst, reduced, mixed))
    mixed = lax.all_gather(mixed, TENSOR, axis=0, tiled=True)
    dfirst = streams(dfirst)


    token_grads, own_mods = [], []
    column_start = lax.axis_index(TENSOR) * columns
    for i in both:
        normed, inverse, _ = firsts[i]
        upstream = dfirst[i]
        token_grads.append(
            middle_grads[i]
            + normalize_back(upstream * (1.0 + modulation[i, :, 1]), normed, inverse)
        )
        gate_one, shift_two, scale_two = statistics[i]
        dmodulation = jnp.stack(
            [
                jnp.sum(upstream, axis=1),
                jnp.sum(upstream * normed, axis=1),
                gate_one,
                shift_two,
                scale_two,
                jnp.sum(cotangents[i].astype(f32), axis=1) * contract_bias[i],
            ],
            axis=1,
        )
        own = lax.dynamic_slice_in_dim(dmodulation, column_start, columns, 2)
        own_mods.append(own.at[:, 5].add(gate_two[i]))
    own_mods = jnp.stack(own_mods).reshape(-1, 128)
    mod_rows = own_mods.shape[0]
    packed = rows_of_lanes(jnp.concatenate([bias_parts[i] for i in range(8)]))
    pieces = exchange(jnp.concatenate([own_mods, packed])[None], PLANE, 8)
    bias_totals = jnp.sum(pieces[:, mod_rows:], axis=0).reshape(-1)
    bias_grads, start = [], 0
    for i in range(8):
        length = bias_parts[i].shape[0]
        bias_grads.append(bias_totals[start : start + length])
        start += length
    own_bias = [lax.dynamic_slice_in_dim(bias_grads[i], own_row, rows_here, 0) for i in range(4)]
    attend_bias_grads = [bias_grads[i].reshape(3, columns)[::2] for i in (4, 5)]
    pieces = pieces[:, :mod_rows].reshape(fsdp_count, heads_count, 2, seqs, 6, columns).sum(axis=1)
    every_mod = pieces.transpose(1, 0, 2, 3, 4).reshape(2, all_seqs, 6, columns)
    row_term = jnp.zeros((all_seqs, rows_here), f32)
    mod_grads, mod_bias_grads = [], []
    for i in both:
        mod_grads.append(
            jnp.einsum("sd,skc->dkc", local_active, every_mod[i], precision=highest)
        )
        mod_bias_grads.append(jnp.sum(every_mod[i], axis=0))
        row_term = row_term + jnp.einsum(
            "skc,dkc->sd", every_mod[i], mod_weights[i].astype(f32), precision=highest
        )
    term_length = seqs * rows_here
    row_term = row_term.reshape(fsdp_count, term_length)
    row_term = jnp.pad(row_term, ((0, 0), (0, rounded_up(term_length, 1024) - term_length)))
    copies = heads_count * tensor_count
    row_term = row_term.reshape(fsdp_count, 1, -1, 128)
    row_term = jnp.broadcast_to(row_term, (fsdp_count, copies) + row_term.shape[2:])
    terms = exchange(row_term.reshape((fsdp_count * copies,) + row_term.shape[2:]), EVERY, 9, scatter=True)
    terms, mixed = lax.optimization_barrier((terms, mixed))
    results, mixed = [], streams(mixed)
    for i in both:
        mixed_rows = mixed[i] + contract_bias[i]
        results.append((seconds[i][0] + modulation[i, :, 5] * mixed_rows).astype(bf16))
    terms = terms.reshape(plane_count, tensor_count, -1)[:, :, :term_length].sum(axis=1)
    dactive = terms.reshape(plane_count, seqs, rows_here).transpose(1, 0, 2).reshape(seqs, width)
    conditioning_gradient = jax.vjp(jax.nn.silu, cond_full)[1](dactive)[0]

    reduced.append(last_reduced)
    order = ((6, 7, 5), (4, 2, 3), (0, 1))
    reduced = [cut(item, [grads[i] for i in keys]) for item, keys in zip(reduced, order)]
    reduced = {i: part for parts, keys in zip(reduced, order) for i, part in zip(keys, parts)}
    shape = latent_attention.shape
    return (
        results[0], results[1][:, :text], token_grads[0], token_grads[1][:, :text],
        conditioning_gradient,
        mod_grads[0], mod_grads[1], mod_bias_grads[0], mod_bias_grads[1],
        reduced[0].reshape(shape), reduced[1].reshape(shape),
        attend_bias_grads[0], attend_bias_grads[1],
        reduced[2], reduced[3], own_bias[0], own_bias[1],
        reduced[4], reduced[5], bias_grads[6], bias_grads[7],
        reduced[6], reduced[7], own_bias[2], own_bias[3],
    )


def solution(mesh):
    rows, tens = P(FSDP, HEADS, None), P(None, TENSOR)
    wide, flat2, line = P(PLANE, None, TENSOR), P(PLANE, TENSOR), P(PLANE)
    hid = P(TENSOR)
    weights = (
        wide, wide, tens, tens, wide, wide, tens, tens, flat2, flat2, line, line,
        flat2, flat2, hid, hid, flat2, flat2, line, line,
    )
    cond = P(FSDP, None)
    in_specs = (rows, rows, cond) + weights + (rows, rows)
    out_specs = (rows, rows, rows, rows, cond) + weights
    return jax.shard_map(body, mesh=mesh, in_specs=in_specs, out_specs=out_specs, check_vma=False)
```

```python
import functools

import jax
import jax.numpy as jnp
from jax import lax
from jax.experimental import pallas as pl
from jax.experimental.pallas import tpu as pltpu
from jax.sharding import PartitionSpec as P

HD = 64
FSDP, HEADS, TENSOR = "fsdp", "heads", "tensor"
PLANE = (FSDP, HEADS)
EVERY = (FSDP, HEADS, TENSOR)
STEP = 32
SKEW = 4
MESH_ID = pl.DeviceIdType.MESH
f32 = jnp.float32
bf16 = jnp.bfloat16
epsilon = 1e-06
highest = lax.Precision.HIGHEST


def normalize(values):
    average = jnp.mean(values, axis=-1, keepdims=True)
    centered = values - average
    variance = jnp.mean(centered * centered, axis=-1, keepdims=True)
    inverse = lax.rsqrt(variance + epsilon)
    return (centered * inverse, inverse)


def normalize_back(upstream, normed, inverse):
    first_mean = jnp.mean(upstream, axis=-1, keepdims=True)
    second_mean = jnp.mean(upstream * normed, axis=-1, keepdims=True)
    return inverse * (upstream - first_mean - normed * second_mean)


def gelu_tanh(values):
    return jax.nn.gelu(values, approximate=True)


def contract(a, b, left, right):
    return lax.dot_general(a, b, (((left,), (right,)), ((), ())), preferred_element_type=f32)


def flat(values):
    return values.reshape(-1, values.shape[-1])


def rounded_up(count, unit):
    return -(-count // unit) * unit


def group_index(axes):
    index = 0
    for name in axes:
        index = index * lax.axis_size(name) + lax.axis_index(name)
    return index


def group_coords(axes, sizes, index):
    coords = {}
    for name, size in reversed(list(zip(axes, sizes))):
        coords[name] = lax.rem(index, size)
        index = index // size
    return coords


def exchange_kernel(axes, sizes, scatter, source, out, send_sems, recv_sems, own_sem):
    total = 1
    for size in sizes:
        total = total * size
    me = 0
    for name, size in zip(axes, sizes):
        me = me * size + lax.axis_index(name)
    barrier = pltpu.get_barrier_semaphore()

    def greet(k, carry):
        peer = lax.rem(me + k, total)
        pl.semaphore_signal(
            barrier, inc=1, device_id=group_coords(axes, sizes, peer), device_id_type=MESH_ID
        )
        return carry

    lax.fori_loop(1, total, greet, 0)
    own = pltpu.make_async_copy(source.at[me if scatter else 0], out.at[me], own_sem)
    own.start()
    pl.semaphore_wait(barrier, total - 1)

    def copy_to(k):
        peer = lax.rem(me + k, total)
        return pltpu.make_async_remote_copy(
            src_ref=source.at[peer if scatter else 0],
            dst_ref=out.at[me],
            send_sem=send_sems.at[k],
            recv_sem=recv_sems.at[k],
            device_id=group_coords(axes, sizes, peer),
            device_id_type=MESH_ID,
        )

    def send(k, carry):
        copy_to(k).start()
        return carry

    lax.fori_loop(1, total, send, 0)

    def receive(k, carry):
        copy_to(k).wait()
        return carry

    lax.fori_loop(1, total, receive, 0)
    own.wait()


def exchange(values, axes, ident, scatter=False):
    sizes = tuple(lax.axis_size(name) for name in axes)
    total = 1
    for size in sizes:
        total = total * size
    block = values.shape[1:]
    vmem = pl.BlockSpec(memory_space=pltpu.VMEM)
    return pl.pallas_call(
        functools.partial(exchange_kernel, axes, sizes, scatter),
        out_shape=jax.ShapeDtypeStruct((total,) + block, values.dtype),
        in_specs=[vmem],
        out_specs=vmem,
        scratch_shapes=[
            pltpu.SemaphoreType.DMA((total,)),
            pltpu.SemaphoreType.DMA((total,)),
            pltpu.SemaphoreType.DMA,
        ],
        compiler_params=pltpu.CompilerParams(collective_id=ident, has_side_effects=True),
        cost_estimate=pl.CostEstimate(flops=1, bytes_accessed=1024, transcendentals=0),
    )(values)


def rows_of_lanes(vector):
    length = vector.shape[0]
    padded = rounded_up(length, 1024)
    return jnp.pad(vector, (0, padded - length)).reshape(padded // 128, 128)


def total_kernel(n, offsets, a0, a1, w_all, out, w0, w1, w_sems, part, land_up, land_down, s_up, r_up, s_down, r_down, bs_up, br_up, bs_down, br_down):
    rows0 = a0.shape[0]
    rows1 = a1.shape[0]
    width = w0.shape[0]
    half = width // 2
    block = 256 if rows0 % 256 == 0 else rows0
    tiles = width // 256
    step = STEP
    per_block = block // step
    count = (rows0 + rows1) // step
    main = rows0 // step
    d = lax.axis_index(TENSOR)

    def tile0(b, t):
        rows = pl.ds(pl.multiple_of(b * block, block), block)
        cols = pl.ds(pl.multiple_of(t * 256, 256), 256)
        part[rows, cols] = contract(a0[rows, :], w0[cols, :], 1, 1).astype(bf16)

    def tile1(t):
        cols = pl.ds(pl.multiple_of(t * 256, 256), 256)
        part[pl.ds(rows0, rows1), cols] = contract(a1[...], w1[cols, :], 1, 1).astype(bf16)

    def rows_of(i):
        return pl.ds(pl.multiple_of(i * step, step), step)

    up_cols = pl.ds(0, half)
    down_cols = pl.ds(half, half)

    def reduce_copy(up, i):
        cols, land, ss, rs = (up_cols, land_up, s_up, r_up) if up else (down_cols, land_down, s_down, r_down)
        return pltpu.make_async_remote_copy(
            src_ref=part.at[rows_of(i), cols],
            dst_ref=land.at[rows_of(i)],
            send_sem=ss.at[i],
            recv_sem=rs.at[i],
            device_id={TENSOR: d + 1 if up else d - 1},
            device_id_type=MESH_ID,
        )

    def spread_copy(up, i):
        cols, ss, rs = (up_cols, bs_up, br_up) if up else (down_cols, bs_down, br_down)
        return pltpu.make_async_remote_copy(
            src_ref=out.at[rows_of(i), cols],
            dst_ref=out.at[rows_of(i), cols],
            send_sem=ss.at[i],
            recv_sem=rs.at[i],
            device_id={TENSOR: d - 1 if up else d + 1},
            device_id_type=MESH_ID,
        )

    def merged(up, i):
        cols, land = (up_cols, land_up) if up else (down_cols, land_down)
        return (part[rows_of(i), cols].astype(f32) + land[rows_of(i), :].astype(f32)).astype(bf16)

    loads = [
        pltpu.make_async_copy(w_all.at[:, pl.ds(offset, w.shape[1])], w, w_sems.at[i])
        for i, (offset, w) in enumerate(zip(offsets, (w0, w1)))
    ]
    for load in loads:
        load.start()
    barrier = pltpu.get_barrier_semaphore()

    @pl.when(d > 0)
    def _():
        pl.semaphore_signal(barrier, inc=1, device_id={TENSOR: d - 1}, device_id_type=MESH_ID)

    @pl.when(d < n - 1)
    def _():
        pl.semaphore_signal(barrier, inc=1, device_id={TENSOR: d + 1}, device_id_type=MESH_ID)

    loads[0].wait()

    def open_tile(t, carry):
        tile0(0, t)
        return carry

    lax.fori_loop(0, tiles, open_tile, 0)
    loads[1].wait()

    ends = (d == 0) | (d == n - 1)

    @pl.when(ends)
    def _():
        pl.semaphore_wait(barrier, 1)

    @pl.when(jnp.logical_not(ends))
    def _():
        pl.semaphore_wait(barrier, 2)

    def by_source(act):
        for up in (True, False):

            @pl.when(d == (0 if up else n - 1))
            def _():
                act(up)

    @pl.when(ends)
    def _():
        def flood(i, carry):
            b = i // per_block
            by_source(lambda up: reduce_copy(up, i).start())

            @pl.when((b + 1 < rows0 // block) & (lax.rem(i, per_block) == 0))
            def _():
                def inner(t, carry):
                    tile0(b + 1, t)
                    return carry

                lax.fori_loop(0, tiles, inner, 0)

            return carry

        lax.fori_loop(0, main, flood, 0)

        def tail_tile(t, carry):
            tile1(t)
            return carry

        lax.fori_loop(0, tiles, tail_tile, 0)

        def flood_tail(i, carry):
            by_source(lambda up: reduce_copy(up, i).start())
            return carry

        lax.fori_loop(main, count, flood_tail, 0)

        def finish(i, carry):
            def act(up):
                other = not up
                reduce_copy(other, i).wait_recv()
                out[rows_of(i), up_cols if other else down_cols] = merged(other, i)
                spread_copy(other, i).start()

            by_source(act)
            return carry

        lax.fori_loop(0, count, finish, 0)

        def gather(i, carry):
            def act(up):
                spread_copy(up, i).wait_recv()
                reduce_copy(up, i).wait_send()
                spread_copy(not up, i).wait_send()

            by_source(act)
            return carry

        lax.fori_loop(0, count, gather, 0)

    @pl.when((d > 0) & (d < n - 1))
    def _():
        def relay(up, i):
            cols = up_cols if up else down_cols
            reduce_copy(up, i).wait_recv()
            part[rows_of(i), cols] = merged(up, i)
            reduce_copy(up, i).start()

        lag = SKEW * (n - 3)
        late_up = SKEW * (d - 1)
        late_down = SKEW * (n - 2 - d)

        def within(i):
            return (i >= 0) & (i < count)

        def pass_on(t, _):
            for up, late in ((True, late_up), (False, late_down)):
                i = t - late

                @pl.when(within(i))
                def _():
                    relay(up, i)

            b = t // per_block
            tile = lax.rem(t, per_block)

            @pl.when((b + 1 < rows0 // block) & (tile < tiles))
            def _():
                tile0(b + 1, tile)

            @pl.when((b + 1 == rows0 // block) & (tile < tiles))
            def _():
                tile1(tile)
            return 0

        lax.fori_loop(0, count + lag, pass_on, 0)

        def spread(t, _):
            for up, late in ((True, late_down), (False, late_up)):
                i = t - late

                @pl.when(within(i))
                def _():
                    spread_copy(up, i).wait_recv()
                    spread_copy(up, i).start()
            return 0

        lax.fori_loop(0, count + lag, spread, 0)

        def drain(i, _):
            for up in (True, False):
                reduce_copy(up, i).wait_send()
                spread_copy(up, i).wait_send()
            return 0

        lax.fori_loop(0, count, drain, 0)


def matmul_total(a0, a1, w_all, offsets, ident):
    n = lax.axis_size(TENSOR)
    rows = a0.shape[0] + a1.shape[0]
    width = w_all.shape[0]
    count = rows // STEP
    depth = a0.shape[1]
    dma = pltpu.SemaphoreType.DMA((count,))
    vmem = pl.BlockSpec(memory_space=pltpu.VMEM)
    return pl.pallas_call(
        functools.partial(total_kernel, n, offsets),
        out_shape=jax.ShapeDtypeStruct((rows, width), bf16),
        in_specs=[vmem, vmem, pl.BlockSpec(memory_space=pl.ANY)],
        out_specs=vmem,
        scratch_shapes=[
            pltpu.VMEM((width, depth), bf16),
            pltpu.VMEM((width, depth), bf16),
            pltpu.SemaphoreType.DMA((2,)),
            pltpu.VMEM((rows, width), bf16),
            pltpu.VMEM((rows, width // 2), bf16),
            pltpu.VMEM((rows, width // 2), bf16),
        ]
        + [dma] * 8,
        compiler_params=pltpu.CompilerParams(
            collective_id=ident, has_side_effects=True, vmem_limit_bytes=56000000
        ),
        cost_estimate=pl.CostEstimate(
            flops=2 * rows * width * a0.shape[1], bytes_accessed=300 * 10**6, transcendentals=0
        ),
    )(a0, a1, w_all)


def query_blocks(main, padded):
    unit = 256 if main % 256 == 0 else 128
    spans = [(start, unit) for start in range(0, main, unit)]
    return spans + [(main, padded - main)]


def key_bias(main, text, valid):
    half = main + text
    row = lax.broadcasted_iota(jnp.int32, (2 * half, 1), 0)
    inside = jnp.where(row >= half, row - half, row)
    return jnp.where(inside >= main + valid, -1e30, 0.0).astype(f32)


def gather_rows(target, pieces, seq, cols):
    start = 0
    for piece in pieces:
        rows = piece.shape[1]
        target[pl.ds(start, rows), :] = piece[seq, :, cols]
        start += rows


def stack_queries(target, main, text, seq, cols, factor):
    lead, tail = main.shape[1], text.shape[1]
    target[pl.ds(0, lead), :] = main[seq, :, cols] * factor
    target[pl.ds(lead, tail), :] = text[seq, :, cols] * factor
    rest = target.shape[0] - lead - tail
    target[pl.ds(lead + tail, rest), :] = jnp.zeros((rest, target.shape[1]), target.dtype)


def lanes_at(pair, offset):
    return pl.ds(pl.multiple_of(pair * 2 * HD + offset, 2 * HD), 2 * HD)


def meet_partner():
    partner = lax.axis_size(HEADS) - 1 - lax.axis_index(HEADS)
    barrier = pltpu.get_barrier_semaphore()
    pl.semaphore_signal(barrier, inc=1, device_id={HEADS: partner}, device_id_type=MESH_ID)
    pl.semaphore_wait(barrier, 1)
    return partner


def head_lanes(head):
    lane = lax.broadcasted_iota(jnp.int32, (1, 2 * HD), 1)
    return (lane >= head * HD) & (lane < (head + 1) * HD)


def attend_kernel(valid, pairs, ti, tt, oi, ot, li, lt, fi, ft, q_all, k_all, v_all, o_all, sends, receives):
    seqs, main, _ = ti.shape
    text = tt.shape[1]
    columns = pairs * 2 * HD
    partner = meet_partner()

    def copies(t):
        seq, pair = t // pairs, lax.rem(t, pairs)
        made = []
        for source, target in ((ti, fi), (tt, ft)):
            for part in range(2):
                which = len(made)
                made.append(
                    pltpu.make_async_remote_copy(
                        src_ref=source.at[seq, :, lanes_at(pair, columns * (1 + part))],
                        dst_ref=target.at[seq, :, lanes_at(pair, columns * part)],
                        send_sem=sends.at[t, which],
                        recv_sem=receives.at[t, which],
                        device_id={HEADS: partner},
                        device_id_type=MESH_ID,
                    )
                )
        return made

    def send(t, carry):
        for copy in copies(t):
            copy.start()
        return carry

    lax.fori_loop(0, seqs * pairs, send, 0)
    bias = key_bias(main, text, valid)

    def step(t, carry):
        seq, pair = t // pairs, lax.rem(t, pairs)
        stack_queries(q_all, ti, tt, seq, lanes_at(pair, 0), jnp.asarray(HD**-0.5, bf16))
        for copy in copies(t):
            copy.wait_recv()
        half = main + text
        for target, part in ((k_all, 0), (v_all, 1)):
            gather_rows(target.at[pl.ds(0, half)], (ti, tt), seq, lanes_at(pair, columns * (1 + part)))
            gather_rows(target.at[pl.ds(half, half)], (fi, ft), seq, lanes_at(pair, columns * part))
        for head in range(2):
            mine = head_lanes(head)
            for start, size in query_blocks(main, q_all.shape[0]):
                queries = jnp.where(mine, q_all[pl.ds(start, size), :], jnp.zeros((), bf16))
                scores = contract(k_all[...], queries, 1, 1) + bias
                top = jnp.max(scores, axis=0, keepdims=True)
                exponent = jnp.exp(scores - top)
                total = jnp.sum(exponent, axis=0, keepdims=True)
                weights = (exponent * (1.0 / total)).astype(bf16)
                attended = contract(v_all[...], weights, 0, 0)
                o_all[pl.ds(head * HD, HD), pl.ds(start, size)] = attended[head * HD : (head + 1) * HD]
                logsum = top + jnp.log(total)
                if start < main:
                    li[seq, pair, pl.ds(head, 1), pl.ds(start, size)] = logsum
                else:
                    lt[seq, pair, pl.ds(head, 1), :] = logsum
        joined = o_all[...].T.astype(bf16)
        oi[seq, :, lanes_at(pair, 0)] = joined[:main]
        ot[seq, :, lanes_at(pair, 0)] = joined[main : main + text]
        return carry

    lax.fori_loop(0, seqs * pairs, step, 0)

    def finish(t, carry):
        for copy in copies(t):
            copy.wait_send()
        return carry

    lax.fori_loop(0, seqs * pairs, finish, 0)


def attend_back_kernel(
    valid, pairs, ti, tt, fi, ft, gi, gt, li, lt, di, dt,
    q_all, k_all, v_all, g_all, dq_all, dk_all, dv_all, own, away_i, away_t, land_i, land_t, sends, receives,
):
    seqs, main, _ = ti.shape
    text = tt.shape[1]
    half = main + text
    columns = pairs * 2 * HD
    partner = meet_partner()

    def copies(t):
        seq, pair = t // pairs, lax.rem(t, pairs)
        made = []
        for source, target in ((away_i, land_i), (away_t, land_t)):
            for part in range(2):
                which = len(made)
                cols = lanes_at(pair, columns * part)
                made.append(
                    pltpu.make_async_remote_copy(
                        src_ref=source.at[seq, :, cols],
                        dst_ref=target.at[seq, :, cols],
                        send_sem=sends.at[t, which],
                        recv_sem=receives.at[t, which],
                        device_id={HEADS: partner},
                        device_id_type=MESH_ID,
                    )
                )
        return made

    bias = key_bias(main, text, valid)

    def step(t, carry):
        seq, pair = t // pairs, lax.rem(t, pairs)
        stack_queries(q_all, ti, tt, seq, lanes_at(pair, 0), jnp.asarray(HD**-0.5, bf16))
        stack_queries(g_all, gi, gt, seq, lanes_at(pair, 0), jnp.asarray(1.0, bf16))
        for target, part in ((k_all, 0), (v_all, 1)):
            gather_rows(target.at[pl.ds(0, half)], (ti, tt), seq, lanes_at(pair, columns * (1 + part)))
            gather_rows(target.at[pl.ds(half, half)], (fi, ft), seq, lanes_at(pair, columns * part))
        first = True
        for head in range(2):
            mine = head_lanes(head)
            for start, size in query_blocks(main, q_all.shape[0]):
                queries = jnp.where(mine, q_all[pl.ds(start, size), :], jnp.zeros((), bf16))
                upstream = jnp.where(mine, g_all[pl.ds(start, size), :], jnp.zeros((), bf16))
                if start < main:
                    logsum = li[seq, pair, pl.ds(head, 1), pl.ds(start, size)]
                else:
                    logsum = lt[seq, pair, pl.ds(head, 1), :]
                weights = jnp.exp(contract(k_all[...], queries, 1, 1) + bias - logsum)
                prob_grads = contract(v_all[...], upstream, 1, 1)
                row_sum = jnp.sum(weights * prob_grads, axis=0, keepdims=True)
                score_grads = (weights * (prob_grads - row_sum)).astype(bf16)
                key_part = contract(score_grads, queries, 1, 0)
                value_part = contract(weights.astype(bf16), upstream, 1, 0)
                if first:
                    dk_all[...] = key_part
                    dv_all[...] = value_part
                else:
                    dk_all[...] += key_part
                    dv_all[...] += value_part
                first = False
                query_part = contract(k_all[...], score_grads, 0, 0)
                dq_all[pl.ds(head * HD, HD), pl.ds(start, size)] = query_part[
                    head * HD : (head + 1) * HD
                ]
        for part, source in ((0, dk_all), (1, dv_all)):
            cols = lanes_at(pair, columns * part)
            away_i[seq, :, cols] = source[pl.ds(half, main), :].astype(bf16)
            away_t[seq, :, cols] = source[pl.ds(half + main, text), :].astype(bf16)
            own[seq, :, cols] = source[pl.ds(0, half), :]
        joined = (dq_all[...].T * HD**-0.5).astype(bf16)
        di[seq, :, lanes_at(pair, 0)] = joined[:main]
        dt[seq, :, lanes_at(pair, 0)] = joined[main : main + text]
        for copy in copies(t):
            copy.start()
        return carry

    lax.fori_loop(0, seqs * pairs, step, 0)

    def finish(t, carry):
        seq, pair = t // pairs, lax.rem(t, pairs)
        for copy in copies(t):
            copy.wait()
        for part in range(2):
            cols = lanes_at(pair, columns * part)
            out_cols = lanes_at(pair, columns * (1 + part))
            mine = own[seq, :, cols]
            di[seq, :, out_cols] = (mine[:main] + land_i[seq, :, cols].astype(f32)).astype(bf16)
            dt[seq, :, out_cols] = (mine[main:] + land_t[seq, :, cols].astype(f32)).astype(bf16)
        return carry

    lax.fori_loop(0, seqs * pairs, finish, 0)


def attention_call(kernel, operands, outputs, scratch, ident, factor):
    seqs, main, columns = operands[0].shape
    pairs = columns // (6 * HD)
    work = seqs * pairs * main * main * 8 * 2 * HD * factor
    vmem = pl.BlockSpec(memory_space=pltpu.VMEM)
    copies = pltpu.SemaphoreType.DMA((seqs * pairs, 4))
    return pl.pallas_call(
        kernel,
        out_shape=outputs,
        in_specs=[vmem] * len(operands),
        out_specs=[vmem] * len(outputs),
        scratch_shapes=scratch + [copies, copies],
        compiler_params=pltpu.CompilerParams(
            collective_id=ident, has_side_effects=True, vmem_limit_bytes=56000000
        ),
        cost_estimate=pl.CostEstimate(flops=work, bytes_accessed=10**7, transcendentals=0),
    )(*operands)


def attend(triples, valid, ident):
    seqs, main, columns = triples[0].shape
    columns = columns // 3
    text = triples[1].shape[1]
    wide = 2 * HD
    pairs = columns // wide
    padded = main + rounded_up(text, 128)
    keys = 2 * (main + text)
    outputs = (
        jax.ShapeDtypeStruct((seqs, main, columns), bf16),
        jax.ShapeDtypeStruct((seqs, text, columns), bf16),
        jax.ShapeDtypeStruct((seqs, pairs, 2, main), f32),
        jax.ShapeDtypeStruct((seqs, pairs, 2, padded - main), f32),
        jax.ShapeDtypeStruct((seqs, main, 2 * columns), bf16),
        jax.ShapeDtypeStruct((seqs, text, 2 * columns), bf16),
    )
    scratch = [
        pltpu.VMEM((padded, wide), bf16),
        pltpu.VMEM((keys, wide), bf16),
        pltpu.VMEM((keys, wide), bf16),
        pltpu.VMEM((wide, padded), f32),
    ]
    kernel = functools.partial(attend_kernel, valid, pairs)
    return attention_call(kernel, tuple(triples), outputs, scratch, ident, 2)


def attend_back(triples, far, upstream, logsums, valid, ident):
    seqs, main, columns = triples[0].shape
    columns = columns // 3
    text = triples[1].shape[1]
    wide = 2 * HD
    pairs = columns // wide
    padded = main + rounded_up(text, 128)
    keys = 2 * (main + text)
    operands = tuple(triples) + tuple(far) + tuple(upstream) + tuple(logsums)
    outputs = tuple(jax.ShapeDtypeStruct(item.shape, bf16) for item in triples)
    scratch = [
        pltpu.VMEM((padded, wide), bf16),
        pltpu.VMEM((keys, wide), bf16),
        pltpu.VMEM((keys, wide), bf16),
        pltpu.VMEM((padded, wide), bf16),
        pltpu.VMEM((wide, padded), f32),
        pltpu.VMEM((keys, wide), f32),
        pltpu.VMEM((keys, wide), f32),
        pltpu.VMEM((seqs, main + text, 2 * columns), f32),
        pltpu.VMEM((seqs, main, 2 * columns), bf16),
        pltpu.VMEM((seqs, text, 2 * columns), bf16),
        pltpu.VMEM((seqs, main, 2 * columns), bf16),
        pltpu.VMEM((seqs, text, 2 * columns), bf16),
    ]
    kernel = functools.partial(attend_back_kernel, valid, pairs)
    return attention_call(kernel, operands, outputs, scratch, ident, 5)


def gathered_rows(shards):
    return lax.all_gather(jnp.concatenate(shards, axis=1), PLANE, axis=0, tiled=True)


def scatter_total(partials):
    partial = jnp.concatenate(partials, axis=1)
    return lax.psum_scatter(partial, PLANE, scatter_dimension=0, tiled=True)


def gate_gradient(partials, columns, ident):
    seqs = partials[0].shape[0]
    sums = jnp.concatenate(partials)
    tensor_count = lax.axis_size(TENSOR)
    sums = sums.reshape(2 * seqs, tensor_count, columns).transpose(1, 0, 2)
    length = 2 * seqs * columns
    sums = sums.reshape(tensor_count, length)
    sums = jnp.pad(sums, ((0, 0), (0, rounded_up(length, 1024) - length)))
    sums = exchange(sums.reshape(tensor_count, -1, 128), (TENSOR,), ident, scatter=True)
    return jnp.sum(sums, axis=0).reshape(-1)[:length].reshape(2, seqs, columns)


def cut(values, like):
    pieces, start = [], 0
    for item in like:
        pieces.append(values[:, start : start + item.shape[1]].astype(f32))
        start += item.shape[1]
    return pieces


def low_product(a, b, left, right):
    return contract(a, b, left, right).astype(bf16)


def body(
    latent_tokens, prompt_tokens, conditioning,
    latent_modulation, prompt_modulation, latent_modulation_bias, prompt_modulation_bias,
    latent_attention, prompt_attention, latent_attention_bias, prompt_attention_bias,
    latent_projection, prompt_projection, latent_projection_bias, prompt_projection_bias,
    latent_expand, prompt_expand, latent_expand_bias, prompt_expand_bias,
    latent_contract, prompt_contract, latent_contract_bias, prompt_contract_bias,
    latent_cotangent, prompt_cotangent,
):
    both = range(2)
    fsdp_count, heads_count = lax.axis_size(FSDP), lax.axis_size(HEADS)
    tensor_count = lax.axis_size(TENSOR)
    plane_count = fsdp_count * heads_count
    seqs, text, width = prompt_tokens.shape
    rows_here = latent_projection.shape[0]
    columns = latent_projection.shape[1]
    all_seqs = seqs * fsdp_count
    padded_text = rounded_up(seqs * text, STEP) // seqs
    while (padded_text * seqs) % STEP or padded_text % 16:
        padded_text += 1
    pad_text = ((0, 0), (0, padded_text - text), (0, 0))
    tokens = (latent_tokens, jnp.pad(prompt_tokens, pad_text))
    cotangents = (latent_cotangent, jnp.pad(prompt_cotangent, pad_text))
    mod_weights = (latent_modulation, prompt_modulation)
    attend_bias = (latent_attention_bias, prompt_attention_bias)
    expand_bias = (latent_expand_bias, prompt_expand_bias)

    third = 3 * columns
    hidden_here = latent_expand.shape[1]
    attend_all = gathered_rows(
        [latent_attention.reshape(rows_here, third), prompt_attention.reshape(rows_here, third)]
    )
    w_attend = [attend_all[:, i * third : (i + 1) * third] for i in both]

    cond_full = conditioning.astype(f32)
    active = jax.nn.silu(cond_full).astype(bf16).astype(f32)
    biases = jnp.concatenate(
        [latent_projection_bias, prompt_projection_bias, latent_contract_bias, prompt_contract_bias]
    ).astype(f32)
    packed = rows_of_lanes(jnp.concatenate([active.reshape(-1), biases]))
    spread = exchange(packed[None], PLANE, 1).reshape(plane_count, -1)
    everyone = spread[:, : seqs * width].reshape(fsdp_count, heads_count, seqs, width)[:, 0]
    everyone = everyone.reshape(all_seqs, width)
    biases = spread[:, seqs * width : seqs * width + 4 * rows_here].reshape(plane_count, 4, rows_here)
    biases = biases.transpose(1, 0, 2).reshape(4, width)
    project_bias, contract_bias = biases[:2], biases[2:]

    own_row = group_index(PLANE) * rows_here
    local_active = lax.dynamic_slice_in_dim(everyone, own_row, rows_here, 1)
    active_low = local_active.astype(bf16)
    parts = jnp.stack([contract(active_low, w, 1, 0) for w in mod_weights])
    parts = parts.reshape(2, fsdp_count, seqs, 6, columns).transpose(1, 0, 2, 3, 4)
    parts = parts.reshape(fsdp_count, 1, -1, 128)
    parts = jnp.broadcast_to(parts, (fsdp_count, heads_count) + parts.shape[2:])
    parts = exchange(parts.reshape((plane_count,) + parts.shape[2:]), PLANE, 2, scatter=True)
    own_mod = jnp.sum(parts, axis=0).reshape(2, seqs, 6, columns)
    mod_bias = jnp.stack([latent_modulation_bias, prompt_modulation_bias]).astype(f32)
    own_mod = (own_mod + mod_bias[:, None]).reshape(1, -1, 128)
    modulation = exchange(own_mod, (TENSOR,), 3).reshape(tensor_count, 2, seqs, 6, columns)
    modulation = modulation.transpose(1, 2, 3, 0, 4).reshape(2, seqs, 6, 1, width)

    firsts, triples = [], []
    for i in both:
        normed, inverse = normalize(tokens[i].astype(f32))
        shifted = (normed * (1.0 + modulation[i, :, 1]) + modulation[i, :, 0]).astype(bf16)
        firsts.append((normed, inverse, flat(shifted)))
    for i in both:
        bias = attend_bias[i].astype(f32)
        offsets = jnp.concatenate([bias[0], jnp.zeros_like(bias[0]), bias[1]])
        triple = contract(firsts[i][2], w_attend[i], 1, 0) + offsets
        triples.append(triple.astype(bf16).reshape(seqs, -1, third))
    project_all = gathered_rows([latent_projection, prompt_projection])
    w_project = [project_all[:, i * columns : (i + 1) * columns] for i in both]
    attended_image, attended_text, *logsums, far_image, far_text = attend(triples, text, 10)
    attended_image, attended_text, wide_shards = lax.optimization_barrier(
        (
            attended_image,
            attended_text,
            [latent_expand, prompt_expand, latent_contract, prompt_contract],
        )
    )
    wide_all = gathered_rows(wide_shards)
    w_wide = [wide_all[:, i * hidden_here : (i + 1) * hidden_here] for i in range(4)]
    w_expand, w_contract = w_wide[:2], w_wide[2:]
    attended = (flat(attended_image), flat(attended_text))
    split = attended[0].shape[0]

    def streams(total):
        return [
            total[:split].reshape(seqs, -1, width).astype(f32),
            total[split:].reshape(seqs, -1, width).astype(f32),
        ]

    projected = streams(matmul_total(
        attended[0], attended[1], project_all, (0, columns), 4
    ))
    projected = [projected[i] + project_bias[i] for i in both]

    seconds, mix_parts = [], []
    for i in both:
        middle = tokens[i].astype(f32) + modulation[i, :, 2] * projected[i]
        normed, inverse = normalize(middle)
        shifted = flat((normed * (1.0 + modulation[i, :, 4]) + modulation[i, :, 3]).astype(bf16))
        upward = contract(shifted, w_expand[i], 1, 0) + expand_bias[i].astype(f32)
        hidden = gelu_tanh(upward).astype(bf16)
        seconds.append((middle, normed, inverse, shifted, upward, hidden))
    gate_parts = []
    for i in both:
        mix = contract(seconds[i][5], w_contract[i], 1, 1)
        mix_parts.append(mix.astype(bf16))
        weighted = cotangents[i].astype(f32) * mix.reshape(seqs, -1, width)
        gate_parts.append(jnp.sum(weighted, axis=1))

    grads, bias_parts, upward_grads = {}, {}, []
    for i in both:
        upward, hidden = seconds[i][4:]
        upstream = cotangents[i].astype(f32)
        dmixed = flat((upstream * modulation[i, :, 5]).astype(bf16))
        dhidden = contract(dmixed, w_contract[i], 1, 0)
        dupward = jax.vjp(gelu_tanh, upward)[1](dhidden)[0].astype(bf16)
        upward_grads.append(dupward)
        grads[i + 6] = low_product(dmixed, hidden, 0, 0)
        bias_parts[i + 2] = jnp.sum(dmixed, axis=0, dtype=f32)
        bias_parts[i + 6] = jnp.sum(dupward, axis=0, dtype=f32)
    grads[5] = low_product(seconds[1][3], upward_grads[1], 0, 0)
    upward_grads, grads = lax.optimization_barrier((upward_grads, grads))
    dsecond = matmul_total(upward_grads[0], upward_grads[1], wide_all, (0, hidden_here), 5)
    reduced = [scatter_total([grads[i] for i in (6, 7, 5)])]
    dsecond, mix_parts, gate_parts, reduced = lax.optimization_barrier(
        (dsecond, mix_parts, gate_parts, reduced)
    )
    dsecond = streams(dsecond)
    mixed = lax.psum_scatter(
        jnp.concatenate(mix_parts), TENSOR, scatter_dimension=0, tiled=True
    )

    statistics, middle_grads, attended_grads, project_grads = [], [], [], []
    for i in both:
        middle, normed, inverse = seconds[i][:3]
        shifts = modulation[i]
        upstream = dsecond[i]
        dmiddle = cotangents[i].astype(f32) + normalize_back(
            upstream * (1.0 + shifts[:, 4]), normed, inverse
        )
        dproject = flat((dmiddle * shifts[:, 2]).astype(bf16))
        attended_grads.append(
            low_product(dproject, w_project[i], 1, 0).reshape(seqs, -1, columns)
        )
        statistics.append(
            [
                jnp.sum(dmiddle * projected[i], axis=1),
                jnp.sum(upstream, axis=1),
                jnp.sum(upstream * normed, axis=1),
            ]
        )
        project_grads.append(dproject)
        bias_parts[i] = jnp.sum(dproject, axis=0, dtype=f32)
        middle_grads.append(dmiddle)

    for i in both:
        grads[i + 2] = low_product(project_grads[i], attended[i], 0, 0)
    grads[4] = low_product(seconds[0][3], upward_grads[0], 0, 0)
    attended_grads, grads = lax.optimization_barrier((attended_grads, grads))
    reduced.append(scatter_total([grads[i] for i in (4, 2, 3)]))
    back = attend_back(triples, (far_image, far_text), attended_grads, logsums, text, 11)
    back, mixed, gate_parts = lax.optimization_barrier((back, mixed, gate_parts))
    gate_two = gate_gradient(gate_parts, columns, 7)
    triple_grads = [flat(item) for item in back]
    for i in both:
        grads[i] = low_product(firsts[i][2], triple_grads[i], 0, 0)
        bias_parts[i + 4] = jnp.sum(triple_grads[i], axis=0, dtype=f32)
    triple_grads, grads = lax.optimization_barrier((triple_grads, grads))
    last_reduced = scatter_total([grads[0], grads[1]])
    dfirst = matmul_total(triple_grads[0], triple_grads[1], attend_all, (0, third), 6)
    dfirst, reduced, mixed = lax.optimization_barrier((dfirst, reduced, mixed))
    mixed = lax.all_gather(mixed, TENSOR, axis=0, tiled=True)
    dfirst = streams(dfirst)


    token_grads, own_mods = [], []
    column_start = lax.axis_index(TENSOR) * columns
    for i in both:
        normed, inverse, _ = firsts[i]
        upstream = dfirst[i]
        token_grads.append(
            middle_grads[i]
            + normalize_back(upstream * (1.0 + modulation[i, :, 1]), normed, inverse)
        )
        gate_one, shift_two, scale_two = statistics[i]
        dmodulation = jnp.stack(
            [
                jnp.sum(upstream, axis=1),
                jnp.sum(upstream * normed, axis=1),
                gate_one,
                shift_two,
                scale_two,
                jnp.sum(cotangents[i].astype(f32), axis=1) * contract_bias[i],
            ],
            axis=1,
        )
        own = lax.dynamic_slice_in_dim(dmodulation, column_start, columns, 2)
        own_mods.append(own.at[:, 5].add(gate_two[i]))
    own_mods, last_reduced = lax.optimization_barrier((own_mods, last_reduced))
    own_mods = jnp.stack(own_mods).reshape(-1, 128)
    mod_rows = own_mods.shape[0]
    packed = rows_of_lanes(jnp.concatenate([bias_parts[i] for i in range(8)]))
    pieces = exchange(jnp.concatenate([own_mods, packed])[None], PLANE, 8)
    bias_totals = jnp.sum(pieces[:, mod_rows:], axis=0).reshape(-1)
    bias_grads, start = [], 0
    for i in range(8):
        length = bias_parts[i].shape[0]
        bias_grads.append(bias_totals[start : start + length])
        start += length
    own_bias = [lax.dynamic_slice_in_dim(bias_grads[i], own_row, rows_here, 0) for i in range(4)]
    attend_bias_grads = [bias_grads[i].reshape(3, columns)[::2] for i in (4, 5)]
    pieces = pieces[:, :mod_rows].reshape(fsdp_count, heads_count, 2, seqs, 6, columns).sum(axis=1)
    every_mod = pieces.transpose(1, 0, 2, 3, 4).reshape(2, all_seqs, 6, columns)
    row_term = jnp.zeros((all_seqs, rows_here), f32)
    mod_grads, mod_bias_grads = [], []
    for i in both:
        mod_grads.append(
            jnp.einsum("sd,skc->dkc", local_active, every_mod[i], precision=highest)
        )
        mod_bias_grads.append(jnp.sum(every_mod[i], axis=0))
        row_term = row_term + jnp.einsum(
            "skc,dkc->sd", every_mod[i], mod_weights[i].astype(f32), precision=highest
        )
    term_length = seqs * rows_here
    row_term = row_term.reshape(fsdp_count, term_length)
    row_term = jnp.pad(row_term, ((0, 0), (0, rounded_up(term_length, 1024) - term_length)))
    copies = heads_count * tensor_count
    row_term = row_term.reshape(fsdp_count, 1, -1, 128)
    row_term = jnp.broadcast_to(row_term, (fsdp_count, copies) + row_term.shape[2:])
    terms = exchange(row_term.reshape((fsdp_count * copies,) + row_term.shape[2:]), EVERY, 9, scatter=True)
    terms, mixed = lax.optimization_barrier((terms, mixed))
    results, mixed = [], streams(mixed)
    for i in both:
        mixed_rows = mixed[i] + contract_bias[i]
        results.append((seconds[i][0] + modulation[i, :, 5] * mixed_rows).astype(bf16))
    terms = terms.reshape(plane_count, tensor_count, -1)[:, :, :term_length].sum(axis=1)
    dactive = terms.reshape(plane_count, seqs, rows_here).transpose(1, 0, 2).reshape(seqs, width)
    conditioning_gradient = jax.vjp(jax.nn.silu, cond_full)[1](dactive)[0]

    reduced.append(last_reduced)
    order = ((6, 7, 5), (4, 2, 3), (0, 1))
    reduced = [cut(item, [grads[i] for i in keys]) for item, keys in zip(reduced, order)]
    reduced = {i: part for parts, keys in zip(reduced, order) for i, part in zip(keys, parts)}
    shape = latent_attention.shape
    return (
        results[0], results[1][:, :text], token_grads[0], token_grads[1][:, :text],
        conditioning_gradient,
        mod_grads[0], mod_grads[1], mod_bias_grads[0], mod_bias_grads[1],
        reduced[0].reshape(shape), reduced[1].reshape(shape),
        attend_bias_grads[0], attend_bias_grads[1],
        reduced[2], reduced[3], own_bias[0], own_bias[1],
        reduced[4], reduced[5], bias_grads[6], bias_grads[7],
        reduced[6], reduced[7], own_bias[2], own_bias[3],
    )


def solution(mesh):
    rows, tens = P(FSDP, HEADS, None), P(None, TENSOR)
    wide, flat2, line = P(PLANE, None, TENSOR), P(PLANE, TENSOR), P(PLANE)
    hid = P(TENSOR)
    weights = (
        wide, wide, tens, tens, wide, wide, tens, tens, flat2, flat2, line, line,
        flat2, flat2, hid, hid, flat2, flat2, line, line,
    )
    cond = P(FSDP, None)
    in_specs = (rows, rows, cond) + weights + (rows, rows)
    out_specs = (rows, rows, rows, rows, cond) + weights
    return jax.shard_map(body, mesh=mesh, in_specs=in_specs, out_specs=out_specs, check_vma=False)
```
